256 devices in a mesh: dp: 8 (over x, core), expert: 8 (over z), mp: 4 (over y).
Axes of the slice: x: 4, y: 4, z: 8, core: 2. Of those that a mesh axis runs over, the one named last changes fastest.
Arguments:
- tokens: bfloat16 [8192, 3072], P(('dp', 'expert'), 'mp'), may hold values from -6 to 6
- expert_ids: int32 [8192, 2], P(('dp', 'expert')), may hold values from 0 to 7, all different within a row; in each aligned block of 128 rows (0 to 127, 128 to 255, ...) at most 36 rows name the same one
- route_weight: bfloat16 [8192, 2], P(('dp', 'expert')), may hold values from 0.099609375 to 1
- w_gate: bfloat16 [8, 3072, 8192], P(None, ('dp', 'expert'), 'mp'), may hold values from -0.109375 to 0.109375
- w_up: bfloat16 [8, 3072, 8192], P(None, ('dp', 'expert'), 'mp'), may hold values from -0.109375 to 0.109375
- grad_hidden: bfloat16 [8, 8, 8, 36, 8192], P('expert', 'dp', None, None, 'mp'), may hold values from -6 to 6
Outputs:
- hidden_out: bfloat16 [8, 8, 8, 36, 8192], P('expert', 'dp', None, None, 'mp')
- grad_tokens: bfloat16 [8192, 3072], P(('dp', 'expert'), 'mp')
The draws below stay inside these ranges and needn't reach their ends.
Inputs may be any that keep to these rules, and one draw needn't show every extreme that they name: `expert_ids`: each row names 2 different experts; among the rows of one token group no expert is named more than 36 times, a bound that some block reaches.
All inputs are finite; a program needn't handle non-finite values.
Results may differ from the reference program's by a relative error of at most 0.0049.
Values may be sent and summed in bfloat16 or wider, within the bound.
A program may use at most 128 MiB of HBM per device.

```python
import math
import jax
import jax.numpy as jnp
import numpy as np
from jax import lax

D = 3072
FF = 8192
TOP = 2
TOK_GRP = 128
E = 8
C = 36
TOKENS = 8192
N_DP = 8
N_EXPERT = 8


def steps_of(rng, shape, cuts, smallest, largest):
    level, own = 1.0, jax.random.fold_in(rng, 6)
    for dim, blocks in cuts:
        heights = jnp.exp(jax.random.uniform(jax.random.fold_in(own, dim), (blocks,), jnp.float32, smallest / len(cuts), largest / len(cuts)))
        level = level * jnp.repeat(heights, shape[dim] // blocks).reshape([-1 if axis == dim else 1 for axis in range(len(shape))])
    return level


def shared_out(rng, own, number, rows, amount, top, limit, lean):
    order = jax.random.permutation(rng, amount)
    packed, ordinary = shares(amount, rows * top, limit, lean, True), shares(amount, rows * top, limit, lean, False)
    places = jnp.arange(amount)

    def named(tallies, rotation):
        used = int((tallies > 0).sum())
        fixed = max(1, used // 4)
        passed = fixed + (places - fixed + rotation * (used - fixed)) % max(1, amount - fixed)
        return jnp.zeros((amount,), jnp.int32).at[order[jnp.where(places < fixed, places, passed)]].set(jnp.asarray(tallies, jnp.int32))

    tallies = jnp.where(number % 4 == 0, named(packed, number // 4), named(ordinary, number - number // 4 - 1))
    mixed = jax.random.permutation(jax.random.fold_in(own, 3), amount)
    giver, receiver = mixed[0:amount // 2 * 2:2], mixed[1:amount // 2 * 2:2]
    slack = jnp.minimum(tallies[giver] - 1, limit - tallies[receiver]) // 2
    slack = jnp.where((giver == order[0]) | (receiver == order[0]) | (tallies[receiver] == 0), 0, jnp.maximum(slack, 0))
    passed = jax.random.randint(jax.random.fold_in(own, 4), (amount // 2,), 0, 1 << 20) % (slack + 1)
    tallies = tallies.at[giver].add(-passed).at[receiver].add(passed)
    labels = jnp.searchsorted(jnp.cumsum(tallies), jnp.arange(rows * top), side="right").astype(jnp.int32)
    listing = labels.reshape(top, rows).T
    listing = listing[jax.random.permutation(jax.random.fold_in(own, 1), rows)]
    rotation = jax.random.randint(jax.random.fold_in(own, 2), (rows, 1), 0, top)
    return jnp.take_along_axis(listing, (jnp.arange(top)[None, :] + rotation) % top, axis=1)


def shares(count, total, most, slope, full):
    weights = [(1 << 20) // math.isqrt(grade ** slope) + 1 for grade in range(1, count + 1)]
    largest = most if full else min(most, max(-(-total // count), total * weights[0] // sum(weights)))
    least = 1 if total - largest >= count - 1 else 0
    holding, spare = [largest] + [least] * (count - 1), total - largest - least * (count - 1)
    while spare > 0:
        free = [i for i in range(1, count) if holding[i] < largest] or [i for i in range(1, count) if holding[i] < most]
        whole, budget = sum([weights[i] for i in free]), spare
        for i in free:
            more = min(most - holding[i], max(1, budget * weights[i] // whole), spare)
            holding[i] = holding[i] + more
            spare = spare - more
    return np.array(holding)


def centred(key, shape, scale, most, pieces=(), kind=jnp.bfloat16):
    entries = scale * jax.random.normal(key, shape, jnp.float32)
    if pieces:
        entries = entries * steps_of(key, shape, pieces, -0.22, 0.18)
    return jnp.clip(entries, -most, most).astype(kind)


def setup_inputs(seed: int = 0) -> dict:
    seeds = jax.random.split(jax.random.key(seed), 7)
    tokens = centred(seeds[0], (TOKENS, D), 1.0, 6.0, ((0, 64), (1, 4)))
    expert_ids_keys = jax.random.split(jax.random.fold_in(seeds[1], 1), TOKENS // TOK_GRP)
    expert_ids_turns = jax.random.permutation(jax.random.fold_in(seeds[1], 3), TOKENS // TOK_GRP)
    expert_ids = jax.vmap(lambda own, number: shared_out(jax.random.fold_in(seeds[1], 2), own, number, TOK_GRP, E, TOP, C, 1))(expert_ids_keys, expert_ids_turns).reshape((TOKENS, TOP))
    route_weight = jnp.clip(jnp.exp(math.log(1.0) - 2.306499 * jax.random.uniform(seeds[2], (TOKENS, TOP), jnp.float32) ** steps_of(seeds[2], (TOKENS, TOP), ((0, 64),), -0.2, 0.2)), 0.099609375, 1.0).astype(jnp.bfloat16)
    w_gate = centred(seeds[3], (E, D, FF), D ** -0.5, 0.109375, ((1, 64), (2, 4)))
    w_up = centred(seeds[4], (E, D, FF), D ** -0.5, 0.109375, ((1, 64), (2, 4)))
    grad_hidden = centred(seeds[5], (E, N_DP, N_EXPERT, C, FF), 1.0, 6.0, ((0, 8), (1, 8), (4, 4)))
    return {"tokens": tokens, "expert_ids": expert_ids, "route_weight": route_weight, "w_gate": w_gate, "w_up": w_up, "grad_hidden": grad_hidden}


def slot_map(expert_ids):
    flat_ids = expert_ids.reshape(-1)
    onehot = (flat_ids[:, None] == jnp.arange(E, dtype=jnp.int32)[None, :]).astype(jnp.int32)
    before = jnp.cumsum(onehot, axis=0) - onehot
    position = jnp.sum(before * onehot, axis=1)
    target = flat_ids * C + position
    placed = target[:, None] == jnp.arange(E * C, dtype=jnp.int32)[None, :]
    return placed.reshape(expert_ids.shape[0], expert_ids.shape[1], E * C)


def expert_pass(inputs):
    slot_rows, slot_scale, gate_w, up_w, grad = inputs
    gate_value = jnp.dot(slot_rows, gate_w, preferred_element_type=jnp.float32)
    up_value = jnp.dot(slot_rows, up_w, preferred_element_type=jnp.float32)
    sigmoid_gate = jax.nn.sigmoid(gate_value)
    weight = slot_scale.astype(jnp.float32)[:, None]
    hidden = (weight * gate_value * sigmoid_gate * up_value).astype(jnp.bfloat16)
    grad_act = weight * grad.astype(jnp.float32)
    gate_grad = (grad_act * up_value * sigmoid_gate * (1.0 + gate_value * (1.0 - sigmoid_gate))).astype(jnp.bfloat16)
    up_grad = (grad_act * gate_value * sigmoid_gate).astype(jnp.bfloat16)
    dims = (((1,), (1,)), ((), ()))
    back_term = lax.dot_general(gate_grad, gate_w, dims, preferred_element_type=jnp.float32)
    back_term = back_term + lax.dot_general(up_grad, up_w, dims, preferred_element_type=jnp.float32)
    return hidden, back_term


def reference(tokens, expert_ids, route_weight, w_gate, w_up, grad_hidden):
    groups = N_DP * N_EXPERT
    tok_blocks = tokens.reshape(groups, TOK_GRP, D).astype(jnp.float32)
    id_blocks = expert_ids.reshape(groups, TOK_GRP, TOP)
    weight_blocks = route_weight.reshape(groups, TOK_GRP, TOP).astype(jnp.float32)
    placed = jax.vmap(slot_map)(id_blocks).astype(jnp.float32)
    select = jnp.sum(placed, axis=2)
    sent_rows = jnp.einsum("gts,gtd->gsd", select, tok_blocks, precision=lax.Precision.HIGHEST).astype(jnp.bfloat16)
    sent_scale = jnp.einsum("gtks,gtk->gs", placed, weight_blocks, precision=lax.Precision.HIGHEST).astype(jnp.bfloat16)
    rows_expert = sent_rows.reshape(groups, E, C, D).transpose(1, 0, 2, 3).reshape(E, groups * C, D)
    scale_expert = sent_scale.reshape(groups, E, C).transpose(1, 0, 2).reshape(E, groups * C)
    grad_expert = grad_hidden.reshape(E, groups * C, FF)
    hidden, back_term = lax.map(expert_pass, (rows_expert, scale_expert, w_gate, w_up, grad_expert))
    hidden_out = hidden.reshape(E, N_DP, N_EXPERT, C, FF)
    back_groups = back_term.reshape(E, groups, C, D).transpose(1, 0, 2, 3).reshape(groups, E * C, D)
    grad_blocks = jnp.einsum("gts,gsd->gtd", select, back_groups, precision=lax.Precision.HIGHEST)
    grad_tokens = grad_blocks.reshape(TOKENS, D).astype(jnp.bfloat16)
    return hidden_out, grad_tokens
```

```python
import functools

import jax
import jax.numpy as jnp
from jax import lax
from jax.experimental import pallas as pl
from jax.experimental.pallas import tpu as pltpu
from jax.sharding import PartitionSpec as P

MESH = pl.DeviceIdType.MESH
UNITS = 128


def slot_map(expert_ids, n_expert, slots_cap):
    flat_ids = expert_ids.reshape(-1)
    onehot = (flat_ids[:, None] == jnp.arange(n_expert, dtype=jnp.int32)[None, :]).astype(jnp.int32)
    before = jnp.cumsum(onehot, axis=0) - onehot
    position = jnp.sum(before * onehot, axis=1)
    target = position * n_expert + flat_ids
    placed = target[:, None] == jnp.arange(n_expert * slots_cap, dtype=jnp.int32)[None, :]
    return placed.reshape(expert_ids.shape[0], expert_ids.shape[1], n_expert * slots_cap)


def stream_kernel(nx, nz, rows_hbm, scale_hbm, gate_hbm, up_hbm, grad_hbm, hid_hbm, back_hbm,
                  stage, wbuf, rows, scale, grad, hid, acc, bsend, brecv,
                  stage_sem, own_sem, z_send, z_recv, x_send, x_recv,
                  in_sem, in_send, in_recv, hid_sem, hid_send, hid_recv, b_send, b_recv, out_sem):
    dp, z, y = lax.axis_index("dp"), lax.axis_index("expert"), lax.axis_index("mp")
    x, c = dp // 2, lax.rem(dp, 2)
    other = 1 - c
    left, right = lax.rem(x + nx - 1, nx), lax.rem(x + 1, nx)
    far = lax.rem(x + 2, nx)
    chunks = wbuf.shape[0]
    part = gate_hbm.shape[1]
    own_rows = part * nz
    chip_rows = 2 * own_rows
    slots = rows.shape[1]
    half_units = chunks * UNITS

    barrier = pltpu.get_barrier_semaphore()
    peers = [(dp - c + cc, lax.rem(z + o, nz), y) for o in range(1, nz) for cc in (0, 1)]
    peers += [(dp - c + other, z, y), (left * 2 + c, z, y), (right * 2 + c, z, y)]
    for peer in peers:
        pl.semaphore_signal(barrier, inc=1, device_id=peer, device_id_type=MESH)

    def stage_copies(k):
        copies = []
        for cc in (0, 1):
            at = pl.multiple_of(cc * half_units + k * UNITS, UNITS)
            copies.append(pltpu.make_async_copy(
                gate_hbm.at[:, :, pl.ds(at, UNITS)], stage.at[k, cc, :, :, pl.ds(0, UNITS)], stage_sem.at[k]))
            copies.append(pltpu.make_async_copy(
                up_hbm.at[:, :, pl.ds(at, UNITS)], stage.at[k, cc, :, :, pl.ds(UNITS, UNITS)], stage_sem.at[k]))
        return copies

    def stage_start(k, _):
        for copy in stage_copies(k):
            copy.start()
        return 0

    lax.fori_loop(0, chunks, stage_start, 0)
    grad_cols = pl.ds(pl.multiple_of(c * half_units, half_units), half_units)
    grad_other = pl.ds(pl.multiple_of(other * half_units, half_units), half_units)
    local_in = [
        pltpu.make_async_copy(rows_hbm, rows.at[c], in_sem.at[0]),
        pltpu.make_async_copy(scale_hbm, scale.at[c], in_sem.at[1]),
        pltpu.make_async_copy(grad_hbm.at[:, grad_cols], grad.at[c], in_sem.at[2]),
    ]
    for copy in local_in:
        copy.start()

    pl.semaphore_wait(barrier, len(peers))

    partner = (dp - c + other, z, y)
    remote_in = [
        pltpu.make_async_remote_copy(rows_hbm, rows.at[c], in_send.at[0], in_recv.at[0], partner, MESH),
        pltpu.make_async_remote_copy(scale_hbm, scale.at[c], in_send.at[1], in_recv.at[1], partner, MESH),
        pltpu.make_async_remote_copy(grad_hbm.at[:, grad_other], grad.at[c], in_send.at[2], in_recv.at[2], partner, MESH),
    ]
    for copy in remote_in:
        copy.start()

    my_block = pl.ds(pl.multiple_of(x * chip_rows + c * own_rows + z * part, 16), part)
    offsets = []
    for o in range(1, nz // 2):
        offsets += [o, nz - o]
    offsets.append(nz // 2)

    def send_z(k, _):
        pltpu.make_async_copy(stage.at[k], stage.at[k], stage_sem.at[k]).wait()
        for o in offsets + [0]:
            zt = lax.rem(z + o, nz)
            for cc in ((c, other) if o else (other,)):
                pltpu.make_async_remote_copy(
                    stage.at[k, cc, zt], wbuf.at[k, my_block, :], z_send.at[k], z_recv.at[k],
                    (dp - c + cc, zt, y), MESH).start()
        pltpu.make_async_copy(stage.at[k, c, z], wbuf.at[k, my_block, :], own_sem.at[k]).start()
        return 0

    lax.fori_loop(0, chunks, send_z, 0)

    def rows_of(chip, first, count):
        return pl.ds(pl.multiple_of(chip * chip_rows + first, 16), count)

    def x_copy(k, way, chip, first, count):
        where = wbuf.at[k, rows_of(chip, first, count), :]
        to = right if way % 2 == 0 else left
        return pltpu.make_async_remote_copy(
            where, where, x_send.at[way, k], x_recv.at[way, k], (to * 2 + c, z, y), MESH)

    n_in = 2 * nz - 1

    def step_own(k):
        whole = wbuf.at[k, pl.ds(0, n_in * part), :]
        pltpu.make_async_copy(whole, whole, z_recv.at[k]).wait()
        pltpu.make_async_copy(stage.at[k, c, z], wbuf.at[k, my_block, :], own_sem.at[k]).wait()
        x_copy(k, 0, x, 0, chip_rows).start()
        x_copy(k, 1, x, 0, chip_rows).start()

    def step_relay(k):
        x_copy(k, 0, left, 0, chip_rows).wait_recv()
        x_copy(k, 2, left, 0, own_rows).start()
        x_copy(k, 1, right, 0, chip_rows).wait_recv()
        x_copy(k, 3, right, own_rows, own_rows).start()

    def hid_out(k):
        cols = pl.ds(pl.multiple_of(c * half_units + k * UNITS, UNITS), UNITS)
        here = pltpu.make_async_copy(hid.at[k, c], hid_hbm.at[:, cols], hid_sem.at[k])
        there = pltpu.make_async_remote_copy(
            hid.at[k, other], hid_hbm.at[:, cols], hid_send.at[k], hid_recv.at[k], partner, MESH)
        return here, there

    def compute(k):
        x_copy(k, 2, far, 0, own_rows).wait_recv()
        x_copy(k, 3, far, own_rows, own_rows).wait_recv()
        at = pl.ds(pl.multiple_of(k * UNITS, UNITS), UNITS)
        both = jnp.dot(rows[...].reshape(2 * slots, rows.shape[2]), wbuf[k], preferred_element_type=jnp.float32)
        gate, up = both[:, :UNITS], both[:, UNITS:]
        weight = scale[...].reshape(2 * slots, UNITS)
        sig = jax.nn.sigmoid(gate)
        hidden = (weight * gate * sig * up).astype(jnp.bfloat16)
        hid[k] = hidden.reshape(2, slots, UNITS)
        grad_act = weight * grad[:, :, at].reshape(2 * slots, UNITS).astype(jnp.float32)
        gate_grad = (grad_act * up * sig * (1.0 + gate * (1.0 - sig))).astype(jnp.bfloat16)
        up_grad = (grad_act * gate * sig).astype(jnp.bfloat16)
        pair = jnp.concatenate([gate_grad, up_grad], axis=1)
        here, there = hid_out(k)
        here.start()
        there.start()
        width = 768

        def back(n, _):
            cols = pl.ds(pl.multiple_of(n * width, width), width)
            term = lax.dot_general(pair, wbuf[k, cols, :], (((1,), (1,)), ((), ())),
                                   preferred_element_type=jnp.float32)
            term = term.reshape(2, slots, width)

            @pl.when(k == 0)
            def _():
                acc[:, :, cols] = term

            @pl.when(k > 0)
            def _():
                acc[:, :, cols] = acc[:, :, cols] + term
            return 0

        lax.fori_loop(0, acc.shape[2] // width, back, 0)

    step_own(0)
    step_own(1)
    step_relay(0)
    for copy in local_in:
        copy.wait()
    pltpu.make_async_copy(rows_hbm, rows.at[other], in_recv.at[0]).wait()
    pltpu.make_async_copy(scale_hbm, scale.at[other], in_recv.at[1]).wait()
    pltpu.make_async_copy(grad_hbm.at[:, grad_other], grad.at[other], in_recv.at[2]).wait()

    def main(k, _):
        @pl.when(k + 2 < chunks)
        def _():
            step_own(k + 2)

        @pl.when(k + 1 < chunks)
        def _():
            step_relay(k + 1)
        compute(k)
        return 0

    lax.fori_loop(0, chunks, main, 0)

    bsend[...] = acc[other].astype(jnp.bfloat16)
    swap = pltpu.make_async_remote_copy(bsend, brecv, b_send, b_recv, partner, MESH)
    swap.start()
    swap.wait()
    bsend[...] = (acc[c] + brecv[...].astype(jnp.float32)).astype(jnp.bfloat16)
    out = pltpu.make_async_copy(bsend, back_hbm, out_sem)
    out.start()

    for copy in remote_in:
        copy.wait_send()

    def drain(k, _):
        whole = wbuf.at[k, pl.ds(0, n_in * part), :]
        pltpu.make_async_copy(whole, whole, z_send.at[k]).wait()
        x_copy(k, 0, x, 0, chip_rows).wait_send()
        x_copy(k, 1, x, 0, chip_rows).wait_send()
        x_copy(k, 2, left, 0, own_rows).wait_send()
        x_copy(k, 3, right, own_rows, own_rows).wait_send()
        here, there = hid_out(k)
        here.wait()
        there.wait_send()
        cols = pl.ds(pl.multiple_of(other * half_units + k * UNITS, UNITS), UNITS)
        pltpu.make_async_copy(hid.at[k, other], hid_hbm.at[:, cols], hid_recv.at[k]).wait()
        return 0

    lax.fori_loop(0, chunks, drain, 0)
    out.wait()


def stream(nx, nz, rows, scale, w_gate, w_up, grad):
    slots, d = rows.shape
    hidden = grad.shape[1]
    chunks = hidden // 2 // UNITS
    part = w_gate.shape[1]
    bf16 = jnp.bfloat16
    dma = pltpu.SemaphoreType.DMA
    return pl.pallas_call(
        functools.partial(stream_kernel, nx, nz),
        out_shape=(jax.ShapeDtypeStruct((slots, hidden), bf16), jax.ShapeDtypeStruct((slots, d), bf16)),
        in_specs=[pl.BlockSpec(memory_space=pl.ANY)] * 5,
        out_specs=[pl.BlockSpec(memory_space=pl.ANY)] * 2,
        scratch_shapes=[
            pltpu.VMEM((chunks, 2, nz, part, 2 * UNITS), bf16),
            pltpu.VMEM((chunks, d, 2 * UNITS), bf16),
            pltpu.VMEM((2, slots, d), bf16),
            pltpu.VMEM((2, slots, UNITS), jnp.float32),
            pltpu.VMEM((2, slots, hidden // 2), bf16),
            pltpu.VMEM((chunks, 2, slots, UNITS), bf16),
            pltpu.VMEM((2, slots, d), jnp.float32),
            pltpu.VMEM((slots, d), bf16),
            pltpu.VMEM((slots, d), bf16),
            dma((chunks,)), dma((chunks,)), dma((chunks,)), dma((chunks,)), dma((4, chunks)), dma((4, chunks)),
            dma((3,)), dma((3,)), dma((3,)), dma((chunks,)), dma((chunks,)), dma((chunks,)), dma(()), dma(()), dma(()),
        ],
        compiler_params=pltpu.CompilerParams(
            collective_id=0, has_side_effects=True, vmem_limit_bytes=60 * 1024 * 1024),
        name="stream",
    )(rows, scale, w_gate, w_up, grad)


def per_device(nx, nz, tokens, expert_ids, route_weight, w_gate, w_up, grad_hidden):
    slots_cap = grad_hidden.shape[3]
    feat = tokens.shape[1]
    hidden_part = w_gate.shape[2]
    slots = nz * slots_cap
    placed = slot_map(expert_ids, nz, slots_cap).astype(jnp.float32)
    select = jnp.sum(placed, axis=1)
    sent_rows = jnp.dot(select.T.astype(jnp.bfloat16), tokens, preferred_element_type=jnp.float32).astype(jnp.bfloat16)
    sent_scale = jnp.einsum("tks,tk->s", placed, route_weight.astype(jnp.float32),
                            precision=lax.Precision.HIGHEST).astype(jnp.bfloat16)
    both = jnp.concatenate([sent_rows, jnp.broadcast_to(sent_scale[:, None], (slots, 128))], axis=1)
    both = both.reshape(slots_cap, nz, feat + 128).transpose(1, 0, 2)
    both = lax.all_to_all(both, "expert", split_axis=0, concat_axis=0, tiled=True)
    both = both.transpose(1, 0, 2).reshape(slots, feat + 128)
    scale = both[:, feat:].astype(jnp.float32)
    rows_full = lax.all_gather(both[:, :feat], "mp", axis=1, tiled=True)
    grad = grad_hidden.transpose(0, 1, 3, 2, 4).reshape(slots, hidden_part)
    hidden, back = stream(nx, nz, rows_full, scale, w_gate, w_up, grad)
    shared = lax.psum_scatter(back, "mp", scatter_dimension=1, tiled=True)
    shared = shared.reshape(slots_cap, nz, feat).transpose(1, 0, 2)
    returned = lax.all_to_all(shared, "expert", split_axis=0, concat_axis=0, tiled=True)
    returned = returned.transpose(1, 0, 2).reshape(slots, feat)
    grad_tokens = jnp.dot(select.astype(jnp.bfloat16), returned, preferred_element_type=jnp.float32)
    hidden_out = hidden.reshape(1, 1, slots_cap, nz, hidden_part).transpose(0, 1, 3, 2, 4)
    return hidden_out, grad_tokens.astype(jnp.bfloat16)


def solution(mesh):
    nx, nz = mesh.shape["dp"] // 2, mesh.shape["expert"]
    in_specs = (
        P(("dp", "expert"), "mp"),
        P(("dp", "expert"), None),
        P(("dp", "expert"), None),
        P(None, ("dp", "expert"), "mp"),
        P(None, ("dp", "expert"), "mp"),
        P("expert", "dp", None, None, "mp"),
    )
    out_specs = (P("expert", "dp", None, None, "mp"), P(("dp", "expert"), "mp"))
    return jax.shard_map(
        functools.partial(per_device, nx, nz), mesh=mesh, in_specs=in_specs, out_specs=out_specs, check_vma=False
    )
```

```python
import functools

import jax
import jax.numpy as jnp
from jax import lax
from jax.experimental import pallas as pl
from jax.experimental.pallas import tpu as pltpu
from jax.sharding import PartitionSpec as P

MESH = pl.DeviceIdType.MESH
UNITS = 128


def slot_map(expert_ids, n_expert, slots_cap):
    flat_ids = expert_ids.reshape(-1)
    onehot = (flat_ids[:, None] == jnp.arange(n_expert, dtype=jnp.int32)[None, :]).astype(jnp.int32)
    before = jnp.cumsum(onehot, axis=0) - onehot
    position = jnp.sum(before * onehot, axis=1)
    target = position * n_expert + flat_ids
    placed = target[:, None] == jnp.arange(n_expert * slots_cap, dtype=jnp.int32)[None, :]
    return placed.reshape(expert_ids.shape[0], expert_ids.shape[1], n_expert * slots_cap)


def stream_kernel(nx, nz, ny, select, planes_hbm, gate_hbm, up_hbm, grad_hbm, hid_hbm, tok_out,
                  stage, wbuf, planes, spread, rows, scale, grad, hid, acc, bsend, brecv, ysend, yrecv, final, zsend, back,
                  stage_sem, own_sem, z_send, z_recv, x_send, x_recv, tok_own, tok_send, tok_recv, y_send, y_recv,
                  in_sem, p_send, p_recv, hid_sem, hid_send, hid_recv, b_send, b_recv, ys_send, ys_recv,
                  r_own, r_send, r_recv):
    dp, z, y = lax.axis_index("dp"), lax.axis_index("expert"), lax.axis_index("mp")
    x, c = dp // 2, lax.rem(dp, 2)
    other = 1 - c
    left, right = lax.rem(x + nx - 1, nx), lax.rem(x + 1, nx)
    far = lax.rem(x + 2, nx)
    y_left, y_right, y_far = lax.rem(y + ny - 1, ny), lax.rem(y + 1, ny), lax.rem(y + 2, ny)
    chunks = wbuf.shape[0]
    part = gate_hbm.shape[1]
    own_rows = part * nz
    chip_rows = 2 * own_rows
    slots = rows.shape[1]
    half = slots // 2
    cap = planes.shape[1]
    feat = tok_out.shape[1]
    lanes = feat // 128
    half_units = chunks * UNITS
    bf16, f32 = jnp.bfloat16, jnp.float32
    partner = (dp - c + other, z, y)

    barrier = pltpu.get_barrier_semaphore()
    peers = [(dp - c + cc, lax.rem(z + o, nz), y) for o in range(1, nz) for cc in (0, 1)]
    peers += [partner, (left * 2 + c, z, y), (right * 2 + c, z, y), (dp, z, y_left), (dp, z, y_right)]
    for peer in peers:
        pl.semaphore_signal(barrier, inc=1, device_id=peer, device_id_type=MESH)

    def stage_copies(k):
        copies = []
        for cc in (0, 1):
            at = pl.multiple_of(cc * half_units + k * UNITS, UNITS)
            copies.append(pltpu.make_async_copy(
                gate_hbm.at[:, :, pl.ds(at, UNITS)], stage.at[k, cc, :, :, pl.ds(0, UNITS)], stage_sem.at[k]))
            copies.append(pltpu.make_async_copy(
                up_hbm.at[:, :, pl.ds(at, UNITS)], stage.at[k, cc, :, :, pl.ds(UNITS, UNITS)], stage_sem.at[k]))
        return copies

    def stage_start(k, _):
        for copy in stage_copies(k):
            copy.start()
        return 0

    lax.fori_loop(0, chunks, stage_start, 0)
    grad_cols = pl.ds(pl.multiple_of(c * half_units, half_units), half_units)
    grad_other = pl.ds(pl.multiple_of(other * half_units, half_units), half_units)
    grad_in = pltpu.make_async_copy(grad_hbm.at[:, grad_cols], grad.at[c], in_sem)
    grad_in.start()
    plane_in = pltpu.make_async_copy(planes_hbm.at[z], planes.at[z], tok_own)
    plane_in.start()

    pl.semaphore_wait(barrier, len(peers))

    my_block = pl.ds(pl.multiple_of(x * chip_rows + c * own_rows + z * part, 16), part)
    offsets = []
    for o in range(1, nz // 2):
        offsets += [o, nz - o]
    offsets.append(nz // 2)

    def send_z(k, _):
        pltpu.make_async_copy(stage.at[k], stage.at[k], stage_sem.at[k]).wait()
        for o in offsets + [0]:
            zt = lax.rem(z + o, nz)
            for cc in ((c, other) if o else (other,)):
                pltpu.make_async_remote_copy(
                    stage.at[k, cc, zt], wbuf.at[k, my_block, :], z_send.at[k], z_recv.at[k],
                    (dp - c + cc, zt, y), MESH).start()
        pltpu.make_async_copy(stage.at[k, c, z], wbuf.at[k, my_block, :], own_sem.at[k]).start()
        return 0

    def plane_out(o):
        zt = lax.rem(z + o, nz)
        return pltpu.make_async_remote_copy(
            planes_hbm.at[zt], planes.at[z], tok_send.at[o - 1], tok_recv.at[z], (dp, zt, y), MESH)

    send_z(0, 0)
    send_z(1, 0)
    for o in offsets:
        plane_out(o).start()
    lax.fori_loop(2, chunks, send_z, 0)

    def to_partner(n, src, dst):
        return pltpu.make_async_remote_copy(src, dst, p_send.at[n], p_recv.at[n], partner, MESH)

    grad_out = to_partner(5, grad_hbm.at[:, grad_other], grad.at[c])
    grad_out.start()

    def rows_of(chip, first, count):
        return pl.ds(pl.multiple_of(chip * chip_rows + first, 16), count)

    def x_copy(k, way, chip, first, count):
        where = wbuf.at[k, rows_of(chip, first, count), :]
        to = right if way % 2 == 0 else left
        return pltpu.make_async_remote_copy(
            where, where, x_send.at[way, k], x_recv.at[way, k], (to * 2 + c, z, y), MESH)

    n_in = 2 * nz - 1

    def step_own(k):
        whole = wbuf.at[k, pl.ds(0, n_in * part), :]
        pltpu.make_async_copy(whole, whole, z_recv.at[k]).wait()
        pltpu.make_async_copy(stage.at[k, c, z], wbuf.at[k, my_block, :], own_sem.at[k]).wait()
        x_copy(k, 0, x, 0, chip_rows).start()
        x_copy(k, 1, x, 0, chip_rows).start()

    def step_relay(k):
        x_copy(k, 0, left, 0, chip_rows).wait_recv()
        x_copy(k, 2, left, 0, own_rows).start()
        x_copy(k, 1, right, 0, chip_rows).wait_recv()
        x_copy(k, 3, right, own_rows, own_rows).start()

    def cols_of(t):
        return pl.ds(pl.multiple_of(t * feat, 128), feat)

    def y_copy(way, t, first, count):
        where = rows.at[c, pl.ds(first, count), cols_of(t)]
        to = y_right if way % 2 == 0 else y_left
        return pltpu.make_async_remote_copy(where, where, y_send.at[way], y_recv.at[way], (dp, z, to), MESH)

    def share(n, t):
        where = rows.at[c, :, cols_of(t)]
        return to_partner(n, where, where)

    def shared(n, t):
        where = rows.at[other, :, cols_of(t)]
        pltpu.make_async_copy(where, where, p_recv.at[n]).wait()

    def gather_rows():
        plane_in.wait()
        for o in offsets:
            zs = lax.rem(z + o, nz)
            pltpu.make_async_copy(planes_hbm.at[zs], planes.at[zs], tok_recv.at[zs]).wait()
        for j in range(nz):
            for n in range(lanes + 1):
                spread[n, pl.ds(j, cap, stride=nz), :] = planes[j, :, n * 128:(n + 1) * 128].astype(f32)
        rows[c, :, cols_of(y)] = jnp.concatenate([spread[n] for n in range(lanes)], axis=1).astype(bf16)
        scale[c] = spread[lanes]
        y_copy(0, y, 0, slots).start()
        y_copy(1, y, 0, slots).start()
        share(0, y).start()
        to_partner(4, scale.at[c], scale.at[c]).start()

    def hid_out(k):
        cols = pl.ds(pl.multiple_of(c * half_units + k * UNITS, UNITS), UNITS)
        here = pltpu.make_async_copy(hid.at[k, c], hid_hbm.at[:, cols], hid_sem.at[k])
        there = pltpu.make_async_remote_copy(
            hid.at[k, other], hid_hbm.at[:, cols], hid_send.at[k], hid_recv.at[k], partner, MESH)
        return here, there

    swaps = (y_far, y_right, y_left, y)

    def swap(n):
        return pltpu.make_async_remote_copy(bsend.at[n], brecv.at[n], b_send.at[n], b_recv.at[n], partner, MESH)

    def compute(k):
        x_copy(k, 2, far, 0, own_rows).wait_recv()
        x_copy(k, 3, far, own_rows, own_rows).wait_recv()
        at = pl.ds(pl.multiple_of(k * UNITS, UNITS), UNITS)
        both = jnp.dot(rows[...].reshape(2 * slots, rows.shape[2]), wbuf[k], preferred_element_type=f32)
        gate, up = both[:, :UNITS], both[:, UNITS:]
        weight = scale[...].reshape(2 * slots, UNITS)
        sig = jax.nn.sigmoid(gate)
        hidden = (weight * gate * sig * up).astype(bf16)
        hid[k] = hidden.reshape(2, slots, UNITS)
        grad_act = weight * grad[:, :, at].reshape(2 * slots, UNITS).astype(f32)
        gate_grad = (grad_act * up * sig * (1.0 + gate * (1.0 - sig))).astype(bf16)
        up_grad = (grad_act * gate * sig).astype(bf16)
        pair = jnp.concatenate([gate_grad, up_grad], axis=1)
        here, there = hid_out(k)
        here.start()
        there.start()
        for n, t in enumerate(swaps):
            cols = cols_of(t)
            term = lax.dot_general(pair, wbuf[k, cols, :], (((1,), (1,)), ((), ())), preferred_element_type=f32)
            term = term.reshape(2, slots, feat)

            @pl.when(k == 0)
            def _():
                acc[:, :, cols] = term

            @pl.when(k > 0)
            def _():
                acc[:, :, cols] = acc[:, :, cols] + term

            @pl.when(k == chunks - 1)
            def _():
                bsend[n] = acc[other, :, cols].astype(bf16)
                swap(n).start()

    step_own(0)
    step_own(1)
    step_relay(0)
    gather_rows()
    step_relay(1)
    y_copy(0, y_left, 0, slots).wait_recv()
    y_copy(2, y_left, 0, half).start()
    share(1, y_left).start()
    y_copy(1, y_right, 0, slots).wait_recv()
    y_copy(3, y_right, half, half).start()
    share(2, y_right).start()
    step_own(2)
    y_copy(2, y_far, 0, half).wait_recv()
    y_copy(3, y_far, half, half).wait_recv()
    share(3, y_far).start()
    grad_in.wait()
    pltpu.make_async_copy(grad_hbm.at[:, grad_other], grad.at[other], p_recv.at[5]).wait()
    pltpu.make_async_copy(scale.at[other], scale.at[other], p_recv.at[4]).wait()
    for n, t in enumerate((y, y_left, y_right, y_far)):
        shared(n, t)

    def main(k, _):
        compute(k)

        @pl.when(k + 3 < chunks)
        def _():
            step_own(k + 3)

        @pl.when(k + 2 < chunks)
        def _():
            step_relay(k + 2)
        return 0

    lax.fori_loop(0, chunks, main, 0)

    upper, lower = pl.ds(0, half), pl.ds(half, half)

    def piece(n):
        to = y_right if n % 2 == 0 else y_left
        return pltpu.make_async_remote_copy(ysend.at[n], yrecv.at[n], ys_send.at[n], ys_recv.at[n], (dp, z, to), MESH)

    def pass_on(n, value):
        ysend[n] = value.astype(bf16)
        piece(n).start()

    swap(0).wait_recv()
    pass_on(0, acc[c, upper, cols_of(y_far)] + brecv[0, upper].astype(f32))
    pass_on(1, acc[c, lower, cols_of(y_far)] + brecv[0, lower].astype(f32))
    swap(1).wait_recv()
    pass_on(2, acc[c, lower, cols_of(y_right)] + brecv[1, lower].astype(f32))
    swap(2).wait_recv()
    pass_on(3, acc[c, upper, cols_of(y_left)] + brecv[2, upper].astype(f32))
    piece(0).wait_recv()
    pass_on(4, acc[c, upper, cols_of(y_right)] + brecv[1, upper].astype(f32) + yrecv[0].astype(f32))
    piece(1).wait_recv()
    pass_on(5, acc[c, lower, cols_of(y_left)] + brecv[2, lower].astype(f32) + yrecv[1].astype(f32))
    swap(3).wait_recv()

    def give_back(h, o):
        zt = lax.rem(z + o, nz)
        return pltpu.make_async_remote_copy(
            zsend.at[h, zt], back.at[h, z], r_send.at[h, o - 1], r_recv.at[h, z], (dp, zt, y), MESH)

    def keep(h):
        return pltpu.make_async_copy(zsend.at[h, z], back.at[h, z], r_own.at[h])

    for h, (near, via) in enumerate(((3, 4), (2, 5))):
        which = (upper, lower)[h]
        piece(near).wait_recv()
        piece(via).wait_recv()
        total = (acc[c, which, cols_of(y)] + brecv[3, which].astype(f32)
                 + yrecv[near].astype(f32) + yrecv[via].astype(f32))
        for n in range(lanes):
            final[n] = total[:, n * 128:(n + 1) * 128]
        for j in range(nz):
            zsend[h, j] = jnp.concatenate(
                [final[n, pl.ds(j, cap // 2, stride=nz), :] for n in range(lanes)], axis=1).astype(bf16)
        for o in offsets:
            give_back(h, o).start()
        keep(h).start()

    def drain(k, _):
        whole = wbuf.at[k, pl.ds(0, n_in * part), :]
        pltpu.make_async_copy(whole, whole, z_send.at[k]).wait()
        x_copy(k, 0, x, 0, chip_rows).wait_send()
        x_copy(k, 1, x, 0, chip_rows).wait_send()
        x_copy(k, 2, left, 0, own_rows).wait_send()
        x_copy(k, 3, right, own_rows, own_rows).wait_send()
        here, there = hid_out(k)
        here.wait()
        there.wait_send()
        cols = pl.ds(pl.multiple_of(other * half_units + k * UNITS, UNITS), UNITS)
        pltpu.make_async_copy(hid.at[k, other], hid_hbm.at[:, cols], hid_recv.at[k]).wait()
        return 0

    lax.fori_loop(0, chunks, drain, 0)
    for o in offsets:
        plane_out(o).wait_send()
    y_copy(0, y, 0, slots).wait_send()
    y_copy(1, y, 0, slots).wait_send()
    y_copy(2, y_left, 0, half).wait_send()
    y_copy(3, y_right, half, half).wait_send()
    for n, t in enumerate((y, y_left, y_right, y_far)):
        share(n, t).wait_send()
    to_partner(4, scale.at[c], scale.at[c]).wait_send()
    grad_out.wait_send()
    for n in range(4):
        swap(n).wait_send()
    for n in range(6):
        piece(n).wait_send()

    for h in (0, 1):
        keep(h).wait()
        for o in offsets:
            zs = lax.rem(z + o, nz)
            pltpu.make_async_copy(zsend.at[h, zs], back.at[h, zs], r_recv.at[h, zs]).wait()
            give_back(h, o).wait_send()
        for e in range(nz):
            for n in range(lanes):
                spread[n, pl.ds(h * half + e, cap // 2, stride=nz), :] = back[h, e, :, n * 128:(n + 1) * 128].astype(f32)
    gathered = jnp.concatenate([spread[n] for n in range(lanes)], axis=1).astype(bf16)
    tok_out[...] = jnp.dot(select[...], gathered, preferred_element_type=f32).astype(bf16)


def stream(nx, nz, ny, select, planes, w_gate, w_up, grad):
    slots, hidden = grad.shape
    cap = planes.shape[1]
    feat = planes.shape[2] - 128
    d = feat * ny
    tokens = select.shape[0]
    chunks = hidden // 2 // UNITS
    part = w_gate.shape[1]
    bf16, f32 = jnp.bfloat16, jnp.float32
    dma = pltpu.SemaphoreType.DMA
    return pl.pallas_call(
        functools.partial(stream_kernel, nx, nz, ny),
        out_shape=(jax.ShapeDtypeStruct((slots, hidden), bf16), jax.ShapeDtypeStruct((tokens, feat), bf16)),
        in_specs=[pl.BlockSpec(memory_space=pltpu.VMEM)] + [pl.BlockSpec(memory_space=pl.ANY)] * 4,
        out_specs=(pl.BlockSpec(memory_space=pl.ANY), pl.BlockSpec(memory_space=pltpu.VMEM)),
        scratch_shapes=[
            pltpu.VMEM((chunks, 2, nz, part, 2 * UNITS), bf16),
            pltpu.VMEM((chunks, d, 2 * UNITS), bf16),
            pltpu.VMEM((nz, cap, feat + 128), bf16),
            pltpu.VMEM((feat // 128 + 1, slots, 128), f32),
            pltpu.VMEM((2, slots, d), bf16),
            pltpu.VMEM((2, slots, UNITS), f32),
            pltpu.VMEM((2, slots, hidden // 2), bf16),
            pltpu.VMEM((chunks, 2, slots, UNITS), bf16),
            pltpu.VMEM((2, slots, d), f32),
            pltpu.VMEM((4, slots, feat), bf16),
            pltpu.VMEM((4, slots, feat), bf16),
            pltpu.VMEM((6, slots // 2, feat), bf16),
            pltpu.VMEM((6, slots // 2, feat), bf16),
            pltpu.VMEM((feat // 128, slots // 2, 128), f32),
            pltpu.VMEM((2, nz, cap // 2, feat), bf16),
            pltpu.VMEM((2, nz, cap // 2, feat), bf16),
            dma((chunks,)), dma((chunks,)), dma((chunks,)), dma((chunks,)), dma((4, chunks)), dma((4, chunks)),
            dma(()), dma((nz - 1,)), dma((nz,)), dma((4,)), dma((4,)),
            dma(()), dma((6,)), dma((6,)), dma((chunks,)), dma((chunks,)), dma((chunks,)),
            dma((4,)), dma((4,)), dma((6,)), dma((6,)),
            dma((2,)), dma((2, nz - 1)), dma((2, nz)),
        ],
        compiler_params=pltpu.CompilerParams(
            collective_id=0, has_side_effects=True, vmem_limit_bytes=62 * 1024 * 1024),
        name="stream",
    )(select, planes, w_gate, w_up, grad)


def per_device(nx, nz, ny, tokens, expert_ids, route_weight, w_gate, w_up, grad_hidden):
    slots_cap = grad_hidden.shape[3]
    feat = tokens.shape[1]
    hidden_part = w_gate.shape[2]
    slots = nz * slots_cap
    placed = slot_map(expert_ids, nz, slots_cap).astype(jnp.float32)
    select = jnp.sum(placed, axis=1)
    by_expert = select.reshape(-1, slots_cap, nz).transpose(2, 1, 0).reshape(slots, -1)
    sent_rows = jnp.dot(by_expert.astype(jnp.bfloat16), tokens, preferred_element_type=jnp.float32).astype(jnp.bfloat16)
    sent_scale = jnp.einsum("tks,tk->s", placed, route_weight.astype(jnp.float32),
                            precision=lax.Precision.HIGHEST).astype(jnp.bfloat16)
    sent_scale = sent_scale.reshape(slots_cap, nz).T.reshape(slots)
    planes = jnp.concatenate([sent_rows, jnp.broadcast_to(sent_scale[:, None], (slots, 128))], axis=1)
    planes = planes.reshape(nz, slots_cap, feat + 128)
    grad = grad_hidden.transpose(0, 1, 3, 2, 4).reshape(slots, hidden_part)
    hidden, grad_tokens = stream(nx, nz, ny, select.astype(jnp.bfloat16), planes, w_gate, w_up, grad)
    hidden_out = hidden.reshape(1, 1, slots_cap, nz, hidden_part).transpose(0, 1, 3, 2, 4)
    return hidden_out, grad_tokens


def solution(mesh):
    nx, nz, ny = mesh.shape["dp"] // 2, mesh.shape["expert"], mesh.shape["mp"]
    in_specs = (
        P(("dp", "expert"), "mp"),
        P(("dp", "expert"), None),
        P(("dp", "expert"), None),
        P(None, ("dp", "expert"), "mp"),
        P(None, ("dp", "expert"), "mp"),
        P("expert", "dp", None, None, "mp"),
    )
    out_specs = (P("expert", "dp", None, None, "mp"), P(("dp", "expert"), "mp"))
    return jax.shard_map(
        functools.partial(per_device, nx, nz, ny), mesh=mesh, in_specs=in_specs, out_specs=out_specs, check_vma=False
    )
```

```python
import functools

import jax
import jax.numpy as jnp
from jax import lax
from jax.experimental import pallas as pl
from jax.experimental.pallas import tpu as pltpu
from jax.sharding import PartitionSpec as P

MESH = pl.DeviceIdType.MESH
UNITS = 128


def slot_map(expert_ids, n_expert, slots_cap):
    flat_ids = expert_ids.reshape(-1)
    onehot = (flat_ids[:, None] == jnp.arange(n_expert, dtype=jnp.int32)[None, :]).astype(jnp.int32)
    before = jnp.cumsum(onehot, axis=0) - onehot
    position = jnp.sum(before * onehot, axis=1)
    target = position * n_expert + flat_ids
    placed = target[:, None] == jnp.arange(n_expert * slots_cap, dtype=jnp.int32)[None, :]
    return placed.reshape(expert_ids.shape[0], expert_ids.shape[1], n_expert * slots_cap)


def stream_kernel(nx, nz, ny, pairs_of, select, planes_hbm, gate_hbm, up_hbm, grad_hbm, hid_hbm, tok_out,
                  stage, wbuf, pairs, planes, spread, rows, scale, grad, hid, acc, bsend, brecv, ysend, yrecv, final, zsend, back,
                  stage_sem, own_sem, z_send, z_recv, x_send, x_recv, tok_own, tok_send, tok_recv, y_send, y_recv,
                  in_sem, p_send, p_recv, hid_sem, hid_send, hid_recv, b_send, b_recv, ys_send, ys_recv,
                  r_own, r_send, r_recv):
    dp, z, y = lax.axis_index("dp"), lax.axis_index("expert"), lax.axis_index("mp")
    x, c = dp // 2, lax.rem(dp, 2)
    other = 1 - c
    left, right = lax.rem(x + nx - 1, nx), lax.rem(x + 1, nx)
    far = lax.rem(x + 2, nx)
    y_left, y_right, y_far = lax.rem(y + ny - 1, ny), lax.rem(y + 1, ny), lax.rem(y + 2, ny)
    chunks = wbuf.shape[0]
    part = gate_hbm.shape[1]
    own_rows = part * nz
    chip_rows = 2 * own_rows
    slots = rows.shape[1]
    half = slots // 2
    cap = planes.shape[1]
    feat = tok_out.shape[1]
    lanes = feat // 128
    half_units = chunks * UNITS
    bf16, f32 = jnp.bfloat16, jnp.float32
    partner = (dp - c + other, z, y)

    barrier = pltpu.get_barrier_semaphore()
    peers = [(dp - c + cc, lax.rem(z + o, nz), y) for o in range(1, nz) for cc in (0, 1)]
    peers += [partner, (left * 2 + c, z, y), (right * 2 + c, z, y), (dp, z, y_left), (dp, z, y_right)]
    for peer in peers:
        pl.semaphore_signal(barrier, inc=1, device_id=peer, device_id_type=MESH)

    def stage_copies(k):
        copies = []
        for cc in (0, 1):
            at = pl.multiple_of(cc * half_units + k * UNITS, UNITS)
            copies.append(pltpu.make_async_copy(
                gate_hbm.at[:, :, pl.ds(at, UNITS)], stage.at[k, cc, :, :, pl.ds(0, UNITS)], stage_sem.at[k]))
            copies.append(pltpu.make_async_copy(
                up_hbm.at[:, :, pl.ds(at, UNITS)], stage.at[k, cc, :, :, pl.ds(UNITS, UNITS)], stage_sem.at[k]))
        return copies

    def stage_start(k, _):
        for copy in stage_copies(k):
            copy.start()
        return 0

    lax.fori_loop(0, chunks, stage_start, 0)
    grad_cols = pl.ds(pl.multiple_of(c * half_units, half_units), half_units)
    grad_other = pl.ds(pl.multiple_of(other * half_units, half_units), half_units)
    grad_in = pltpu.make_async_copy(grad_hbm.at[:, grad_cols], grad.at[c], in_sem)
    grad_in.start()
    plane_in = pltpu.make_async_copy(planes_hbm.at[z], planes.at[z], tok_own)
    plane_in.start()

    pl.semaphore_wait(barrier, len(peers))

    my_block = pl.ds(pl.multiple_of(x * chip_rows + c * own_rows + z * part, 16), part)
    across = nz // 2
    early = 4
    offsets = [across]
    for o in range(across - 1, 0, -1):
        offsets += [o, nz - o]

    def send_z(k, _):
        pltpu.make_async_copy(stage.at[k], stage.at[k], stage_sem.at[k]).wait()
        for o in offsets + [0]:
            zt = lax.rem(z + o, nz)
            for cc in ((c, other) if o else (other,)):
                pltpu.make_async_remote_copy(
                    stage.at[k, cc, zt], wbuf.at[k, my_block, :], z_send.at[k], z_recv.at[k],
                    (dp - c + cc, zt, y), MESH).start()
        pltpu.make_async_copy(stage.at[k, c, z], wbuf.at[k, my_block, :], own_sem.at[k]).start()
        return 0

    def plane_out(o):
        zt = lax.rem(z + o, nz)
        return pltpu.make_async_remote_copy(
            planes_hbm.at[zt], planes.at[z], tok_send.at[o - 1], tok_recv.at[z], (dp, zt, y), MESH)

    pltpu.make_async_copy(stage.at[0], stage.at[0], stage_sem.at[0]).wait()
    pltpu.make_async_copy(stage.at[0, c, z], wbuf.at[0, my_block, :], own_sem.at[0]).start()
    for part_of in (0, 1):
        lane = pl.ds(part_of * UNITS, UNITS)
        slot = part_of * chunks
        for o in offsets + [0]:
            zt = lax.rem(z + o, nz)
            for cc in ((c, other) if o else (other,)):
                pltpu.make_async_remote_copy(
                    stage.at[0, cc, zt, :, lane], wbuf.at[0, my_block, lane], z_send.at[slot], z_recv.at[slot],
                    (dp - c + cc, zt, y), MESH).start()
    lax.fori_loop(1, early, send_z, 0)
    for o in offsets:
        plane_out(o).start()
    lax.fori_loop(early, chunks, send_z, 0)

    def to_partner(n, src, dst):
        return pltpu.make_async_remote_copy(src, dst, p_send.at[n], p_recv.at[n], partner, MESH)

    grad_out = to_partner(5, grad_hbm.at[:, grad_other], grad.at[c])
    grad_out.start()

    def rows_of(chip, first, count):
        return pl.ds(pl.multiple_of(chip * chip_rows + first, 16), count)

    def x_copy(k, way, chip, first, count, part_of=None):
        lane = pl.ds(0, 2 * UNITS) if part_of is None else pl.ds(part_of * UNITS, UNITS)
        slot = chunks if part_of == 1 else k
        where = wbuf.at[k, rows_of(chip, first, count), lane]
        to = right if way % 2 == 0 else left
        return pltpu.make_async_remote_copy(
            where, where, x_send.at[way, slot], x_recv.at[way, slot], (to * 2 + c, z, y), MESH)

    n_in = 2 * nz - 1

    def step_own(k):
        whole = wbuf.at[k, pl.ds(0, n_in * part), :]
        pltpu.make_async_copy(whole, whole, z_recv.at[k]).wait()
        pltpu.make_async_copy(stage.at[k, c, z], wbuf.at[k, my_block, :], own_sem.at[k]).wait()
        x_copy(k, 0, x, 0, chip_rows).start()
        x_copy(k, 1, x, 0, chip_rows).start()

    def step_relay(k, part_of=None):
        x_copy(k, 0, left, 0, chip_rows, part_of).wait_recv()
        x_copy(k, 2, left, 0, own_rows, part_of).start()
        x_copy(k, 1, right, 0, chip_rows, part_of).wait_recv()
        x_copy(k, 3, right, own_rows, own_rows, part_of).start()

    def first_own(part_of):
        whole = wbuf.at[0, pl.ds(0, n_in * part), pl.ds(part_of * UNITS, UNITS)]
        pltpu.make_async_copy(whole, whole, z_recv.at[part_of * chunks]).wait()
        x_copy(0, 0, x, 0, chip_rows, part_of).start()
        x_copy(0, 1, x, 0, chip_rows, part_of).start()

    def cols_of(t):
        return pl.ds(pl.multiple_of(t * feat, 128), feat)

    def y_copy(way, t, first, count):
        where = rows.at[c, pl.ds(first, count), cols_of(t)]
        to = y_right if way % 2 == 0 else y_left
        return pltpu.make_async_remote_copy(where, where, y_send.at[way], y_recv.at[way], (dp, z, to), MESH)

    def share(n, t):
        where = rows.at[c, :, cols_of(t)]
        return to_partner(n, where, where)

    def shared(n, t):
        where = rows.at[other, :, cols_of(t)]
        pltpu.make_async_copy(where, where, p_recv.at[n]).wait()

    def gather_rows():
        plane_in.wait()
        for o in offsets:
            zs = lax.rem(z + o, nz)
            pltpu.make_async_copy(planes_hbm.at[zs], planes.at[zs], tok_recv.at[zs]).wait()
        for j in range(nz):
            for n in range(lanes + 1):
                spread[n, pl.ds(j, cap, stride=nz), :] = planes[j, :, n * 128:(n + 1) * 128].astype(f32)
        rows[c, :, cols_of(y)] = jnp.concatenate([spread[n] for n in range(lanes)], axis=1).astype(bf16)
        scale[c] = spread[lanes]
        y_copy(0, y, 0, slots).start()
        y_copy(1, y, 0, slots).start()
        share(0, y).start()
        to_partner(4, scale.at[c], scale.at[c]).start()

    def hid_out(k):
        cols = pl.ds(pl.multiple_of(c * half_units + k * UNITS, UNITS), UNITS)
        here = pltpu.make_async_copy(hid.at[k, c], hid_hbm.at[:, cols], hid_sem.at[k])
        there = pltpu.make_async_remote_copy(
            hid.at[k, other], hid_hbm.at[:, cols], hid_send.at[k], hid_recv.at[k], partner, MESH)
        return here, there

    swaps = (y_far, y_right, y_left, y)

    def swap(n):
        return pltpu.make_async_remote_copy(bsend.at[n], brecv.at[n], b_send.at[n], b_recv.at[n], partner, MESH)

    def compute(k):
        @pl.when(k > 0)
        def _():
            x_copy(k, 2, far, 0, own_rows).wait_recv()
            x_copy(k, 3, far, own_rows, own_rows).wait_recv()
        at = pl.ds(pl.multiple_of(k * UNITS, UNITS), UNITS)
        both = jnp.dot(rows[...].reshape(2 * slots, rows.shape[2]), wbuf[k], preferred_element_type=f32)
        gate, up = both[:, :UNITS], both[:, UNITS:]
        weight = scale[...].reshape(2 * slots, UNITS)
        sig = jax.nn.sigmoid(gate)
        hidden = (weight * gate * sig * up).astype(bf16)
        hid[k] = hidden.reshape(2, slots, UNITS)
        grad_act = weight * grad[:, :, at].reshape(2 * slots, UNITS).astype(f32)
        gate_grad = (grad_act * up * sig * (1.0 + gate * (1.0 - sig))).astype(bf16)
        up_grad = (grad_act * gate * sig).astype(bf16)
        pairs[:, :UNITS] = gate_grad
        pairs[:, UNITS:] = up_grad
        here, there = hid_out(k)
        here.start()
        there.start()

        def backward(n, _):
            cols = cols_of(lax.rem(y + 2 + 3 * n + 3 * (n // 2) + 2 * (n // 3), ny))
            term = lax.dot_general(pairs[...], wbuf[k, cols, :], (((1,), (1,)), ((), ())), preferred_element_type=f32)
            acc[:, :, cols] += term.reshape(2, slots, feat)

            @pl.when(k == chunks - 1)
            def _():
                bsend[n] = acc[other, :, cols].astype(bf16)
                swap(n).start()
            return 0

        lax.fori_loop(0, ny, backward, 0)

    acc[...] = jnp.zeros_like(acc)
    pltpu.make_async_copy(stage.at[0, c, z], wbuf.at[0, my_block, :], own_sem.at[0]).wait()
    first_own(0)
    first_own(1)
    step_relay(0, 0)
    step_relay(0, 1)
    step_own(1)
    step_own(2)
    step_relay(1)
    step_own(3)
    step_relay(2)
    gather_rows()
    step_relay(3)
    step_own(4)
    y_copy(0, y_left, 0, slots).wait_recv()
    y_copy(2, y_left, 0, half).start()
    share(1, y_left).start()
    y_copy(1, y_right, 0, slots).wait_recv()
    y_copy(3, y_right, half, half).start()
    share(2, y_right).start()
    step_own(5)
    y_copy(2, y_far, 0, half).wait_recv()
    y_copy(3, y_far, half, half).wait_recv()
    share(3, y_far).start()
    grad_in.wait()
    pltpu.make_async_copy(grad_hbm.at[:, grad_other], grad.at[other], p_recv.at[5]).wait()
    pltpu.make_async_copy(scale.at[other], scale.at[other], p_recv.at[4]).wait()
    for n, t in enumerate((y, y_left, y_right, y_far)):
        shared(n, t)

    for part_of in (0, 1):
        x_copy(0, 2, far, 0, own_rows, part_of).wait_recv()
        x_copy(0, 3, far, own_rows, own_rows, part_of).wait_recv()

    def main(k, _):
        compute(k)

        @pl.when(k == 0)
        def _():
            step_relay(4)
            step_own(6)

        @pl.when(k == 2)
        def _():
            step_relay(5)
            step_own(7)

        @pl.when(k == 4)
        def _():
            step_relay(6)

        @pl.when(k == 5)
        def _():
            step_relay(7)
        return 0

    lax.fori_loop(0, chunks, main, 0)

    subs = 2 * pairs_of
    sub = slots // subs
    per = cap // pairs_of

    def piece(kind, n):
        to = y_right if (n + kind) % 2 == 0 else y_left
        at = (kind // 2) * subs + n if kind % 2 == 0 else 2 * subs + n
        return pltpu.make_async_remote_copy(
            ysend.at[at], yrecv.at[at], ys_send.at[at], ys_recv.at[at], (dp, z, to), MESH)

    def got(kind, n):
        at = (kind // 2) * subs + n if kind % 2 == 0 else 2 * subs + n
        piece(kind, n).wait_recv()
        return yrecv[at].astype(f32)

    def pass_on(kind, n, value):
        at = (kind // 2) * subs + n if kind % 2 == 0 else 2 * subs + n
        ysend[at] = value.astype(bf16)
        piece(kind, n).start()

    def mine(order, n):
        rows_n = pl.ds(n * sub, sub)
        return acc[c, rows_n, cols_of(swaps[order])] + brecv[order, rows_n].astype(f32)

    swap(0).wait_recv()
    for n in range(subs):
        pass_on(0, n, mine(0, n))
    swap(1).wait_recv()
    swap(2).wait_recv()
    for g in range(pairs_of):
        for n in (2 * g + 1, 2 * g):
            pass_on(1, n, mine(1 if n % 2 else 2, n))
        for n in (2 * g, 2 * g + 1):
            pass_on(2, n, mine(2 if n % 2 else 1, n) + got(0, n))
    swap(3).wait_recv()

    def give_back(g, o):
        zt = lax.rem(z + o, nz)
        return pltpu.make_async_remote_copy(
            zsend.at[g, zt], back.at[g, z], r_send.at[g, o - 1], r_recv.at[g, z], (dp, zt, y), MESH)

    def keep(g):
        return pltpu.make_async_copy(zsend.at[g, z], back.at[g, z], r_own.at[g])

    for g in range(pairs_of):
        for i in (0, 1):
            n = 2 * g + i
            total = mine(3, n) + got(1, n) + got(2, n)
            for m in range(lanes):
                final[m, pl.ds(i * sub, sub), :] = total[:, m * 128:(m + 1) * 128]
        for j in range(nz):
            zsend[g, j] = jnp.concatenate(
                [final[m, pl.ds(j, per, stride=nz), :] for m in range(lanes)], axis=1).astype(bf16)
        for o in offsets:
            give_back(g, o).start()
        keep(g).start()

    def sent(k, part_of):
        x_copy(k, 0, x, 0, chip_rows, part_of).wait_send()
        x_copy(k, 1, x, 0, chip_rows, part_of).wait_send()
        x_copy(k, 2, left, 0, own_rows, part_of).wait_send()
        x_copy(k, 3, right, own_rows, own_rows, part_of).wait_send()

    for part_of in (0, 1):
        whole = wbuf.at[0, pl.ds(0, n_in * part), pl.ds(part_of * UNITS, UNITS)]
        pltpu.make_async_copy(whole, whole, z_send.at[part_of * chunks]).wait()
        sent(0, part_of)

    def drain(k, _):
        @pl.when(k > 0)
        def _():
            whole = wbuf.at[k, pl.ds(0, n_in * part), :]
            pltpu.make_async_copy(whole, whole, z_send.at[k]).wait()
            sent(k, None)
        here, there = hid_out(k)
        here.wait()
        there.wait_send()
        cols = pl.ds(pl.multiple_of(other * half_units + k * UNITS, UNITS), UNITS)
        pltpu.make_async_copy(hid.at[k, other], hid_hbm.at[:, cols], hid_recv.at[k]).wait()
        return 0

    lax.fori_loop(0, chunks, drain, 0)
    for o in offsets:
        plane_out(o).wait_send()
    y_copy(0, y, 0, slots).wait_send()
    y_copy(1, y, 0, slots).wait_send()
    y_copy(2, y_left, 0, half).wait_send()
    y_copy(3, y_right, half, half).wait_send()
    for n, t in enumerate((y, y_left, y_right, y_far)):
        share(n, t).wait_send()
    to_partner(4, scale.at[c], scale.at[c]).wait_send()
    grad_out.wait_send()
    for n in range(4):
        swap(n).wait_send()
    for kind in range(3):
        for n in range(subs):
            piece(kind, n).wait_send()

    result = jnp.zeros(tok_out.shape, f32)
    for g in range(pairs_of):
        keep(g).wait()
        for o in offsets:
            zs = lax.rem(z + o, nz)
            pltpu.make_async_copy(zsend.at[g, zs], back.at[g, zs], r_recv.at[g, zs]).wait()
        for e in range(nz):
            for m in range(lanes):
                spread[m, pl.ds(2 * g * sub + e, per, stride=nz), :] = back[g, e, :, m * 128:(m + 1) * 128].astype(f32)
        rows_g = pl.ds(2 * g * sub, 2 * sub)
        gathered = jnp.concatenate([spread[m, rows_g, :] for m in range(lanes)], axis=1).astype(bf16)
        result += lax.dot_general(select[rows_g, :], gathered, (((0,), (0,)), ((), ())), preferred_element_type=f32)
    for g in range(pairs_of):
        for o in offsets:
            give_back(g, o).wait_send()
    tok_out[...] = result.astype(bf16)


def stream(nx, nz, ny, select, planes, w_gate, w_up, grad):
    slots, hidden = grad.shape
    cap = planes.shape[1]
    feat = planes.shape[2] - 128
    d = feat * ny
    tokens = select.shape[1]
    pairs_of = 3
    chunks = hidden // 2 // UNITS
    part = w_gate.shape[1]
    bf16, f32 = jnp.bfloat16, jnp.float32
    dma = pltpu.SemaphoreType.DMA
    return pl.pallas_call(
        functools.partial(stream_kernel, nx, nz, ny, pairs_of),
        out_shape=(jax.ShapeDtypeStruct((slots, hidden), bf16), jax.ShapeDtypeStruct((tokens, feat), bf16)),
        in_specs=[pl.BlockSpec(memory_space=pltpu.VMEM)] + [pl.BlockSpec(memory_space=pl.ANY)] * 4,
        out_specs=(pl.BlockSpec(memory_space=pl.ANY), pl.BlockSpec(memory_space=pltpu.VMEM)),
        scratch_shapes=[
            pltpu.VMEM((chunks, 2, nz, part, 2 * UNITS), bf16),
            pltpu.VMEM((chunks, d, 2 * UNITS), bf16),
            pltpu.VMEM((2 * slots, 2 * UNITS), bf16),
            pltpu.VMEM((nz, cap, feat + 128), bf16),
            pltpu.VMEM((feat // 128 + 1, slots, 128), f32),
            pltpu.VMEM((2, slots, d), bf16),
            pltpu.VMEM((2, slots, UNITS), f32),
            pltpu.VMEM((2, slots, hidden // 2), bf16),
            pltpu.VMEM((chunks, 2, slots, UNITS), bf16),
            pltpu.VMEM((2, slots, d), f32),
            pltpu.VMEM((4, slots, feat), bf16),
            pltpu.VMEM((4, slots, feat), bf16),
            pltpu.VMEM((6 * pairs_of, slots // (2 * pairs_of), feat), bf16),
            pltpu.VMEM((6 * pairs_of, slots // (2 * pairs_of), feat), bf16),
            pltpu.VMEM((feat // 128, slots // pairs_of, 128), f32),
            pltpu.VMEM((pairs_of, nz, cap // pairs_of, feat), bf16),
            pltpu.VMEM((pairs_of, nz, cap // pairs_of, feat), bf16),
            dma((chunks,)), dma((chunks,)), dma((chunks + 1,)), dma((chunks + 1,)),
            dma((4, chunks + 1)), dma((4, chunks + 1)),
            dma(()), dma((nz - 1,)), dma((nz,)), dma((4,)), dma((4,)),
            dma(()), dma((6,)), dma((6,)), dma((chunks,)), dma((chunks,)), dma((chunks,)),
            dma((4,)), dma((4,)), dma((6 * pairs_of,)), dma((6 * pairs_of,)),
            dma((pairs_of,)), dma((pairs_of, nz - 1)), dma((pairs_of, nz)),
        ],
        compiler_params=pltpu.CompilerParams(
            collective_id=0, has_side_effects=True, vmem_limit_bytes=62 * 1024 * 1024),
        name="stream",
    )(select, planes, w_gate, w_up, grad)


def per_device(nx, nz, ny, tokens, expert_ids, route_weight, w_gate, w_up, grad_hidden):
    slots_cap = grad_hidden.shape[3]
    feat = tokens.shape[1]
    hidden_part = w_gate.shape[2]
    slots = nz * slots_cap
    placed = slot_map(expert_ids, nz, slots_cap).astype(jnp.float32)
    select = jnp.sum(placed, axis=1)
    by_expert = select.reshape(-1, slots_cap, nz).transpose(2, 1, 0).reshape(slots, -1)
    sent_rows = jnp.dot(by_expert.astype(jnp.bfloat16), tokens, preferred_element_type=jnp.float32).astype(jnp.bfloat16)
    sent_scale = jnp.einsum("tks,tk->s", placed, route_weight.astype(jnp.float32),
                            precision=lax.Precision.HIGHEST).astype(jnp.bfloat16)
    sent_scale = sent_scale.reshape(slots_cap, nz).T.reshape(slots)
    planes = jnp.concatenate([sent_rows, jnp.broadcast_to(sent_scale[:, None], (slots, 128))], axis=1)
    planes = planes.reshape(nz, slots_cap, feat + 128)
    grad = grad_hidden.transpose(0, 1, 3, 2, 4).reshape(slots, hidden_part)
    hidden, grad_tokens = stream(nx, nz, ny, select.T.astype(jnp.bfloat16), planes, w_gate, w_up, grad)
    hidden_out = hidden.reshape(1, 1, slots_cap, nz, hidden_part).transpose(0, 1, 3, 2, 4)
    return hidden_out, grad_tokens


def solution(mesh):
    nx, nz, ny = mesh.shape["dp"] // 2, mesh.shape["expert"], mesh.shape["mp"]
    in_specs = (
        P(("dp", "expert"), "mp"),
        P(("dp", "expert"), None),
        P(("dp", "expert"), None),
        P(None, ("dp", "expert"), "mp"),
        P(None, ("dp", "expert"), "mp"),
        P("expert", "dp", None, None, "mp"),
    )
    out_specs = (P("expert", "dp", None, None, "mp"), P(("dp", "expert"), "mp"))
    return jax.shard_map(
        functools.partial(per_device, nx, nz, ny), mesh=mesh, in_specs=in_specs, out_specs=out_specs, check_vma=False
    )
```

```python
import functools

import jax
import jax.numpy as jnp
from jax import lax
from jax.experimental import pallas as pl
from jax.experimental.pallas import tpu as pltpu
from jax.sharding import PartitionSpec as P

MESH = pl.DeviceIdType.MESH
UNITS = 128


def stream_kernel(nx, nz, ny, pairs_of, ids, weights, tok_hbm, gate_hbm, up_hbm, grad_hbm, hid_hbm, tok_out,
                  stage, wbuf, pairs, tok, chosen, select, own_planes, planes, spread, rows, scale, grad, hid, acc, bsend, brecv, ysend, yrecv, final, zsend, back,
                  stage_sem, own_sem, z_send, z_recv, x_send, x_recv, tok_in, tok_own, tok_send, tok_recv, y_send, y_recv,
                  in_sem, p_send, p_recv, hid_sem, hid_send, hid_recv, b_send, b_recv, ys_send, ys_recv,
                  r_own, r_send, r_recv):
    dp, z, y = lax.axis_index("dp"), lax.axis_index("expert"), lax.axis_index("mp")
    x, c = dp // 2, lax.rem(dp, 2)
    other = 1 - c
    left, right = lax.rem(x + nx - 1, nx), lax.rem(x + 1, nx)
    far = lax.rem(x + 2, nx)
    y_left, y_right, y_far = lax.rem(y + ny - 1, ny), lax.rem(y + 1, ny), lax.rem(y + 2, ny)
    chunks = wbuf.shape[0]
    part = gate_hbm.shape[1]
    own_rows = part * nz
    chip_rows = 2 * own_rows
    slots = rows.shape[1]
    half = slots // 2
    cap = planes.shape[1]
    feat = tok_out.shape[1]
    lanes = feat // 128
    padded = chosen.shape[0] // nz
    half_units = chunks * UNITS
    bf16, f32 = jnp.bfloat16, jnp.float32
    partner = (dp - c + other, z, y)

    barrier = pltpu.get_barrier_semaphore()
    peers = [(dp - c + cc, lax.rem(z + o, nz), y) for o in range(1, nz) for cc in (0, 1)]
    peers += [partner, (left * 2 + c, z, y), (right * 2 + c, z, y), (dp, z, y_left), (dp, z, y_right)]
    for peer in peers:
        pl.semaphore_signal(barrier, inc=1, device_id=peer, device_id_type=MESH)

    def stage_copies(k):
        copies = []
        for cc in (0, 1):
            at = pl.multiple_of(cc * half_units + k * UNITS, UNITS)
            copies.append(pltpu.make_async_copy(
                gate_hbm.at[:, :, pl.ds(at, UNITS)], stage.at[k, cc, :, :, pl.ds(0, UNITS)], stage_sem.at[k]))
            copies.append(pltpu.make_async_copy(
                up_hbm.at[:, :, pl.ds(at, UNITS)], stage.at[k, cc, :, :, pl.ds(UNITS, UNITS)], stage_sem.at[k]))
        return copies

    def stage_start(k, _):
        for copy in stage_copies(k):
            copy.start()
        return 0

    lax.fori_loop(0, chunks, stage_start, 0)
    grad_cols = pl.ds(pl.multiple_of(c * half_units, half_units), half_units)
    grad_other = pl.ds(pl.multiple_of(other * half_units, half_units), half_units)
    grad_in = pltpu.make_async_copy(grad_hbm.at[:, grad_cols], grad.at[c], in_sem)
    grad_in.start()
    tokens_in = pltpu.make_async_copy(tok_hbm, tok, tok_in)
    tokens_in.start()
    plane_in = pltpu.make_async_copy(own_planes.at[z], planes.at[z], tok_own)

    pl.semaphore_wait(barrier, len(peers))

    my_block = pl.ds(pl.multiple_of(x * chip_rows + c * own_rows + z * part, 16), part)
    across = nz // 2
    early = 4
    offsets = [across]
    for o in range(across - 1, 0, -1):
        offsets += [o, nz - o]

    def send_z(k, _):
        pltpu.make_async_copy(stage.at[k], stage.at[k], stage_sem.at[k]).wait()
        for o in offsets + [0]:
            zt = lax.rem(z + o, nz)
            for cc in ((c, other) if o else (other,)):
                pltpu.make_async_remote_copy(
                    stage.at[k, cc, zt], wbuf.at[k, my_block, :], z_send.at[k], z_recv.at[k],
                    (dp - c + cc, zt, y), MESH).start()
        pltpu.make_async_copy(stage.at[k, c, z], wbuf.at[k, my_block, :], own_sem.at[k]).start()
        return 0

    def dispatch():
        tokens = tok.shape[0]
        expert = lax.broadcasted_iota(jnp.int32, (nz, tokens), 0)
        first, second = ids[0:1, :] == expert, ids[1:2, :] == expert
        named = jnp.where(first | second, 1.0, 0.0)
        route = jnp.where(first, weights[0:1, :], 0.0) + jnp.where(second, weights[1:2, :], 0.0)
        earlier = (lax.broadcasted_iota(jnp.int32, (tokens, tokens), 0)
                   < lax.broadcasted_iota(jnp.int32, (tokens, tokens), 1))
        before = jnp.dot(named.astype(bf16), jnp.where(earlier, 1.0, 0.0).astype(bf16), preferred_element_type=f32)
        place = jnp.where(named > 0.5, before, -1.0).astype(jnp.int32)
        slot = lax.broadcasted_iota(jnp.int32, (padded, tokens), 0)
        for e in range(nz):
            picked = jnp.where(slot == place[e:e + 1, :], 1.0, 0.0)
            chosen[pl.ds(e * padded, padded), :] = picked.astype(bf16)
            select[pl.ds(e, cap, stride=nz), :] = picked[:cap]
            factor = jnp.sum(picked[:cap] * route[e:e + 1, :], axis=1, keepdims=True)
            own_planes[e, :, feat:] = jnp.broadcast_to(factor, (cap, 128)).astype(bf16)
        tokens_in.wait()
        taken = jnp.dot(chosen[...], tok[...], preferred_element_type=f32).astype(bf16)
        for e in range(nz):
            own_planes[e, :, :feat] = taken[e * padded:e * padded + cap, :]

    def plane_out(o):
        zt = lax.rem(z + o, nz)
        return pltpu.make_async_remote_copy(
            own_planes.at[zt], planes.at[z], tok_send.at[o - 1], tok_recv.at[z], (dp, zt, y), MESH)

    pltpu.make_async_copy(stage.at[0], stage.at[0], stage_sem.at[0]).wait()
    pltpu.make_async_copy(stage.at[0, c, z], wbuf.at[0, my_block, :], own_sem.at[0]).start()
    for part_of in (0, 1):
        lane = pl.ds(part_of * UNITS, UNITS)
        slot = part_of * chunks
        for o in offsets + [0]:
            zt = lax.rem(z + o, nz)
            for cc in ((c, other) if o else (other,)):
                pltpu.make_async_remote_copy(
                    stage.at[0, cc, zt, :, lane], wbuf.at[0, my_block, lane], z_send.at[slot], z_recv.at[slot],
                    (dp - c + cc, zt, y), MESH).start()
    dispatch()
    lax.fori_loop(1, early, send_z, 0)
    plane_in.start()
    for o in offsets:
        plane_out(o).start()
    lax.fori_loop(early, chunks, send_z, 0)

    def to_partner(n, src, dst):
        return pltpu.make_async_remote_copy(src, dst, p_send.at[n], p_recv.at[n], partner, MESH)

    grad_out = to_partner(5, grad_hbm.at[:, grad_other], grad.at[c])
    grad_out.start()

    def rows_of(chip, first, count):
        return pl.ds(pl.multiple_of(chip * chip_rows + first, 16), count)

    def x_copy(k, way, chip, first, count, part_of=None):
        lane = pl.ds(0, 2 * UNITS) if part_of is None else pl.ds(part_of * UNITS, UNITS)
        slot = chunks if part_of == 1 else k
        where = wbuf.at[k, rows_of(chip, first, count), lane]
        to = right if way % 2 == 0 else left
        return pltpu.make_async_remote_copy(
            where, where, x_send.at[way, slot], x_recv.at[way, slot], (to * 2 + c, z, y), MESH)

    n_in = 2 * nz - 1

    def step_own(k):
        whole = wbuf.at[k, pl.ds(0, n_in * part), :]
        pltpu.make_async_copy(whole, whole, z_recv.at[k]).wait()
        pltpu.make_async_copy(stage.at[k, c, z], wbuf.at[k, my_block, :], own_sem.at[k]).wait()
        x_copy(k, 0, x, 0, chip_rows).start()
        x_copy(k, 1, x, 0, chip_rows).start()

    def step_relay(k, part_of=None):
        x_copy(k, 0, left, 0, chip_rows, part_of).wait_recv()
        x_copy(k, 2, left, 0, own_rows, part_of).start()
        x_copy(k, 1, right, 0, chip_rows, part_of).wait_recv()
        x_copy(k, 3, right, own_rows, own_rows, part_of).start()

    def first_own(part_of):
        whole = wbuf.at[0, pl.ds(0, n_in * part), pl.ds(part_of * UNITS, UNITS)]
        pltpu.make_async_copy(whole, whole, z_recv.at[part_of * chunks]).wait()
        x_copy(0, 0, x, 0, chip_rows, part_of).start()
        x_copy(0, 1, x, 0, chip_rows, part_of).start()

    def cols_of(t):
        return pl.ds(pl.multiple_of(t * feat, 128), feat)

    def y_copy(way, t, first, count):
        where = rows.at[c, pl.ds(first, count), cols_of(t)]
        to = y_right if way % 2 == 0 else y_left
        return pltpu.make_async_remote_copy(where, where, y_send.at[way], y_recv.at[way], (dp, z, to), MESH)

    def share(n, t):
        where = rows.at[c, :, cols_of(t)]
        return to_partner(n, where, where)

    def shared(n, t):
        where = rows.at[other, :, cols_of(t)]
        pltpu.make_async_copy(where, where, p_recv.at[n]).wait()

    def gather_rows():
        plane_in.wait()
        for o in offsets:
            zs = lax.rem(z + o, nz)
            pltpu.make_async_copy(own_planes.at[zs], planes.at[zs], tok_recv.at[zs]).wait()
        for j in range(nz):
            for n in range(lanes + 1):
                spread[n, pl.ds(j, cap, stride=nz), :] = planes[j, :, n * 128:(n + 1) * 128].astype(f32)
        rows[c, :, cols_of(y)] = jnp.concatenate([spread[n] for n in range(lanes)], axis=1).astype(bf16)
        scale[c] = spread[lanes]
        y_copy(0, y, 0, slots).start()
        y_copy(1, y, 0, slots).start()
        share(0, y).start()
        to_partner(4, scale.at[c], scale.at[c]).start()

    def hid_out(k):
        cols = pl.ds(pl.multiple_of(c * half_units + k * UNITS, UNITS), UNITS)
        here = pltpu.make_async_copy(hid.at[k, c], hid_hbm.at[:, cols], hid_sem.at[k])
        there = pltpu.make_async_remote_copy(
            hid.at[k, other], hid_hbm.at[:, cols], hid_send.at[k], hid_recv.at[k], partner, MESH)
        return here, there

    swaps = (y_far, y_right, y_left, y)

    def swap(n):
        return pltpu.make_async_remote_copy(bsend.at[n], brecv.at[n], b_send.at[n], b_recv.at[n], partner, MESH)

    def compute(k):
        @pl.when(k > 0)
        def _():
            x_copy(k, 2, far, 0, own_rows).wait_recv()
            x_copy(k, 3, far, own_rows, own_rows).wait_recv()
        at = pl.ds(pl.multiple_of(k * UNITS, UNITS), UNITS)
        both = jnp.dot(rows[...].reshape(2 * slots, rows.shape[2]), wbuf[k], preferred_element_type=f32)
        gate, up = both[:, :UNITS], both[:, UNITS:]
        weight = scale[...].reshape(2 * slots, UNITS)
        sig = jax.nn.sigmoid(gate)
        hidden = (weight * gate * sig * up).astype(bf16)
        hid[k] = hidden.reshape(2, slots, UNITS)
        grad_act = weight * grad[:, :, at].reshape(2 * slots, UNITS).astype(f32)
        gate_grad = (grad_act * up * sig * (1.0 + gate * (1.0 - sig))).astype(bf16)
        up_grad = (grad_act * gate * sig).astype(bf16)
        pairs[:, :UNITS] = gate_grad
        pairs[:, UNITS:] = up_grad
        here, there = hid_out(k)
        here.start()
        there.start()

        def backward(n, _):
            cols = cols_of(lax.rem(y + 2 + 3 * n + 3 * (n // 2) + 2 * (n // 3), ny))
            term = lax.dot_general(pairs[...], wbuf[k, cols, :], (((1,), (1,)), ((), ())), preferred_element_type=f32)
            acc[:, :, cols] += term.reshape(2, slots, feat)

            @pl.when(k == chunks - 1)
            def _():
                bsend[n] = acc[other, :, cols].astype(bf16)
                swap(n).start()
            return 0

        lax.fori_loop(0, ny, backward, 0)

    acc[...] = jnp.zeros_like(acc)
    pltpu.make_async_copy(stage.at[0, c, z], wbuf.at[0, my_block, :], own_sem.at[0]).wait()
    first_own(0)
    first_own(1)
    step_relay(0, 0)
    step_relay(0, 1)
    step_own(1)
    step_own(2)
    step_relay(1)
    step_own(3)
    step_relay(2)
    gather_rows()
    step_relay(3)
    step_own(4)
    y_copy(0, y_left, 0, slots).wait_recv()
    y_copy(2, y_left, 0, half).start()
    share(1, y_left).start()
    y_copy(1, y_right, 0, slots).wait_recv()
    y_copy(3, y_right, half, half).start()
    share(2, y_right).start()
    step_own(5)
    y_copy(2, y_far, 0, half).wait_recv()
    y_copy(3, y_far, half, half).wait_recv()
    share(3, y_far).start()
    grad_in.wait()
    pltpu.make_async_copy(grad_hbm.at[:, grad_other], grad.at[other], p_recv.at[5]).wait()
    pltpu.make_async_copy(scale.at[other], scale.at[other], p_recv.at[4]).wait()
    for n, t in enumerate((y, y_left, y_right, y_far)):
        shared(n, t)

    for part_of in (0, 1):
        x_copy(0, 2, far, 0, own_rows, part_of).wait_recv()
        x_copy(0, 3, far, own_rows, own_rows, part_of).wait_recv()

    def main(k, _):
        compute(k)

        @pl.when(k == 0)
        def _():
            step_relay(4)
            step_own(6)

        @pl.when(k == 2)
        def _():
            step_relay(5)
            step_own(7)

        @pl.when(k == 4)
        def _():
            step_relay(6)

        @pl.when(k == 5)
        def _():
            step_relay(7)
        return 0

    lax.fori_loop(0, chunks, main, 0)

    subs = 2 * pairs_of
    sub = slots // subs
    per = cap // pairs_of

    def piece(kind, n):
        to = y_right if (n + kind) % 2 == 0 else y_left
        at = (kind // 2) * subs + n if kind % 2 == 0 else 2 * subs + n
        return pltpu.make_async_remote_copy(
            ysend.at[at], yrecv.at[at], ys_send.at[at], ys_recv.at[at], (dp, z, to), MESH)

    def got(kind, n):
        at = (kind // 2) * subs + n if kind % 2 == 0 else 2 * subs + n
        piece(kind, n).wait_recv()
        return yrecv[at].astype(f32)

    def pass_on(kind, n, value):
        at = (kind // 2) * subs + n if kind % 2 == 0 else 2 * subs + n
        ysend[at] = value.astype(bf16)
        piece(kind, n).start()

    def mine(order, n):
        rows_n = pl.ds(n * sub, sub)
        return acc[c, rows_n, cols_of(swaps[order])] + brecv[order, rows_n].astype(f32)

    swap(0).wait_recv()
    for n in range(subs):
        pass_on(0, n, mine(0, n))
    swap(1).wait_recv()
    swap(2).wait_recv()
    for g in range(pairs_of):
        for n in (2 * g + 1, 2 * g):
            pass_on(1, n, mine(1 if n % 2 else 2, n))
        for n in (2 * g, 2 * g + 1):
            pass_on(2, n, mine(2 if n % 2 else 1, n) + got(0, n))
    swap(3).wait_recv()

    def give_back(g, o):
        zt = lax.rem(z + o, nz)
        return pltpu.make_async_remote_copy(
            zsend.at[g, zt], back.at[g, z], r_send.at[g, o - 1], r_recv.at[g, z], (dp, zt, y), MESH)

    def keep(g):
        return pltpu.make_async_copy(zsend.at[g, z], back.at[g, z], r_own.at[g])

    for g in range(pairs_of):
        for i in (0, 1):
            n = 2 * g + i
            total = mine(3, n) + got(1, n) + got(2, n)
            for m in range(lanes):
                final[m, pl.ds(i * sub, sub), :] = total[:, m * 128:(m + 1) * 128]
        for j in range(nz):
            zsend[g, j] = jnp.concatenate(
                [final[m, pl.ds(j, per, stride=nz), :] for m in range(lanes)], axis=1).astype(bf16)
        for o in offsets:
            give_back(g, o).start()
        keep(g).start()

    def sent(k, part_of):
        x_copy(k, 0, x, 0, chip_rows, part_of).wait_send()
        x_copy(k, 1, x, 0, chip_rows, part_of).wait_send()
        x_copy(k, 2, left, 0, own_rows, part_of).wait_send()
        x_copy(k, 3, right, own_rows, own_rows, part_of).wait_send()

    for part_of in (0, 1):
        whole = wbuf.at[0, pl.ds(0, n_in * part), pl.ds(part_of * UNITS, UNITS)]
        pltpu.make_async_copy(whole, whole, z_send.at[part_of * chunks]).wait()
        sent(0, part_of)

    def drain(k, _):
        @pl.when(k > 0)
        def _():
            whole = wbuf.at[k, pl.ds(0, n_in * part), :]
            pltpu.make_async_copy(whole, whole, z_send.at[k]).wait()
            sent(k, None)
        here, there = hid_out(k)
        here.wait()
        there.wait_send()
        cols = pl.ds(pl.multiple_of(other * half_units + k * UNITS, UNITS), UNITS)
        pltpu.make_async_copy(hid.at[k, other], hid_hbm.at[:, cols], hid_recv.at[k]).wait()
        return 0

    lax.fori_loop(0, chunks, drain, 0)
    for o in offsets:
        plane_out(o).wait_send()
    y_copy(0, y, 0, slots).wait_send()
    y_copy(1, y, 0, slots).wait_send()
    y_copy(2, y_left, 0, half).wait_send()
    y_copy(3, y_right, half, half).wait_send()
    for n, t in enumerate((y, y_left, y_right, y_far)):
        share(n, t).wait_send()
    to_partner(4, scale.at[c], scale.at[c]).wait_send()
    grad_out.wait_send()
    for n in range(4):
        swap(n).wait_send()
    for kind in range(3):
        for n in range(subs):
            piece(kind, n).wait_send()

    result = jnp.zeros(tok_out.shape, f32)
    for g in range(pairs_of):
        keep(g).wait()
        for o in offsets:
            zs = lax.rem(z + o, nz)
            pltpu.make_async_copy(zsend.at[g, zs], back.at[g, zs], r_recv.at[g, zs]).wait()
        for e in range(nz):
            for m in range(lanes):
                spread[m, pl.ds(2 * g * sub + e, per, stride=nz), :] = back[g, e, :, m * 128:(m + 1) * 128].astype(f32)
        rows_g = pl.ds(2 * g * sub, 2 * sub)
        gathered = jnp.concatenate([spread[m, rows_g, :] for m in range(lanes)], axis=1).astype(bf16)
        result += lax.dot_general(select[rows_g, :].astype(bf16), gathered, (((0,), (0,)), ((), ())), preferred_element_type=f32)
    for g in range(pairs_of):
        for o in offsets:
            give_back(g, o).wait_send()
    tok_out[...] = result.astype(bf16)


def stream(nx, nz, ny, cap, ids, weights, tokens, w_gate, w_up, grad):
    slots, hidden = grad.shape
    count, feat = tokens.shape
    padded = -(-cap // 16) * 16
    d = feat * ny
    pairs_of = 3
    chunks = hidden // 2 // UNITS
    part = w_gate.shape[1]
    bf16, f32 = jnp.bfloat16, jnp.float32
    dma = pltpu.SemaphoreType.DMA
    return pl.pallas_call(
        functools.partial(stream_kernel, nx, nz, ny, pairs_of),
        out_shape=(pltpu.VMEM((slots, hidden), bf16), pltpu.VMEM((count, feat), bf16)),
        in_specs=[pl.BlockSpec(memory_space=pltpu.VMEM)] * 2 + [pl.BlockSpec(memory_space=pl.ANY)] * 4,
        out_specs=(pl.BlockSpec(memory_space=pltpu.VMEM), pl.BlockSpec(memory_space=pltpu.VMEM)),
        scratch_shapes=[
            pltpu.VMEM((chunks, 2, nz, part, 2 * UNITS), bf16),
            pltpu.VMEM((chunks, d, 2 * UNITS), bf16),
            pltpu.VMEM((2 * slots, 2 * UNITS), bf16),
            pltpu.VMEM((count, feat), bf16),
            pltpu.VMEM((nz * padded, count), bf16),
            pltpu.VMEM((slots, count), f32),
            pltpu.VMEM((nz, cap, feat + 128), bf16),
            pltpu.VMEM((nz, cap, feat + 128), bf16),
            pltpu.VMEM((feat // 128 + 1, slots, 128), f32),
            pltpu.VMEM((2, slots, d), bf16),
            pltpu.VMEM((2, slots, UNITS), f32),
            pltpu.VMEM((2, slots, hidden // 2), bf16),
            pltpu.VMEM((chunks, 2, slots, UNITS), bf16),
            pltpu.VMEM((2, slots, d), f32),
            pltpu.VMEM((4, slots, feat), bf16),
            pltpu.VMEM((4, slots, feat), bf16),
            pltpu.VMEM((6 * pairs_of, slots // (2 * pairs_of), feat), bf16),
            pltpu.VMEM((6 * pairs_of, slots // (2 * pairs_of), feat), bf16),
            pltpu.VMEM((feat // 128, slots // pairs_of, 128), f32),
            pltpu.VMEM((pairs_of, nz, cap // pairs_of, feat), bf16),
            pltpu.VMEM((pairs_of, nz, cap // pairs_of, feat), bf16),
            dma((chunks,)), dma((chunks,)), dma((chunks + 1,)), dma((chunks + 1,)),
            dma((4, chunks + 1)), dma((4, chunks + 1)),
            dma(()), dma(()), dma((nz - 1,)), dma((nz,)), dma((4,)), dma((4,)),
            dma(()), dma((6,)), dma((6,)), dma((chunks,)), dma((chunks,)), dma((chunks,)),
            dma((4,)), dma((4,)), dma((6 * pairs_of,)), dma((6 * pairs_of,)),
            dma((pairs_of,)), dma((pairs_of, nz - 1)), dma((pairs_of, nz)),
        ],
        compiler_params=pltpu.CompilerParams(
            collective_id=0, has_side_effects=True, vmem_limit_bytes=62 * 1024 * 1024),
        name="stream",
    )(ids, weights, tokens, w_gate, w_up, grad)


def per_device(nx, nz, ny, tokens, expert_ids, route_weight, w_gate, w_up, grad_hidden):
    slots_cap = grad_hidden.shape[3]
    hidden_part = w_gate.shape[2]
    slots = nz * slots_cap
    grad = grad_hidden.transpose(0, 1, 3, 2, 4).reshape(slots, hidden_part)
    hidden, grad_tokens = stream(nx, nz, ny, slots_cap, expert_ids.T, route_weight.T.astype(jnp.float32),
                                 tokens, w_gate, w_up, grad)
    hidden_out = hidden.reshape(1, 1, slots_cap, nz, hidden_part).transpose(0, 1, 3, 2, 4)
    return hidden_out, grad_tokens


def solution(mesh):
    nx, nz, ny = mesh.shape["dp"] // 2, mesh.shape["expert"], mesh.shape["mp"]
    in_specs = (
        P(("dp", "expert"), "mp"),
        P(("dp", "expert"), None),
        P(("dp", "expert"), None),
        P(None, ("dp", "expert"), "mp"),
        P(None, ("dp", "expert"), "mp"),
        P("expert", "dp", None, None, "mp"),
    )
    out_specs = (P("expert", "dp", None, None, "mp"), P(("dp", "expert"), "mp"))
    return jax.shard_map(
        functools.partial(per_device, nx, nz, ny), mesh=mesh, in_specs=in_specs, out_specs=out_specs, check_vma=False
    )
```

```python
import functools

import jax
import jax.numpy as jnp
from jax import lax
from jax.experimental import pallas as pl
from jax.experimental.pallas import tpu as pltpu
from jax.sharding import PartitionSpec as P

MESH = pl.DeviceIdType.MESH
UNITS = 128


def stream_kernel(nx, nz, ny, pairs_of, ids, weights, tok_hbm, gate_hbm, up_hbm, grad_hbm, hid_hbm, tok_out,
                  stage, wbuf, pairs, tok, chosen, select, own_planes, planes, spread, rows, scale, grad, hid, acc, bsend, brecv, ysend, yrecv, final, zsend, back,
                  stage_sem, own_sem, d_send, d_recv, f_send, f_recv, z_send, z_recv, x_send, x_recv, tok_in, tok_own, tok_send, tok_recv, y_send, y_recv,
                  in_sem, p_send, p_recv, hid_sem, hid_send, hid_recv, b_send, b_recv, ys_send, ys_recv,
                  r_own, r_send, r_recv):
    dp, z, y = lax.axis_index("dp"), lax.axis_index("expert"), lax.axis_index("mp")
    x, c = dp // 2, lax.rem(dp, 2)
    other = 1 - c
    left, right = lax.rem(x + nx - 1, nx), lax.rem(x + 1, nx)
    far = lax.rem(x + 2, nx)
    y_left, y_right, y_far = lax.rem(y + ny - 1, ny), lax.rem(y + 1, ny), lax.rem(y + 2, ny)
    chunks = wbuf.shape[0]
    part = gate_hbm.shape[1]
    own_rows = part * nz
    chip_rows = 2 * own_rows
    slots = rows.shape[1]
    half = slots // 2
    cap = planes.shape[1]
    feat = tok_out.shape[1]
    lanes = feat // 128
    padded = chosen.shape[0] // nz
    half_units = chunks * UNITS
    bf16, f32 = jnp.bfloat16, jnp.float32
    partner = (dp - c + other, z, y)

    barrier = pltpu.get_barrier_semaphore()
    peers = [(dp - c + cc, lax.rem(z + o, nz), y) for o in range(1, nz) for cc in (0, 1)]
    peers += [partner, (left * 2 + c, z, y), (right * 2 + c, z, y), (dp, z, y_left), (dp, z, y_right)]
    for peer in peers:
        pl.semaphore_signal(barrier, inc=1, device_id=peer, device_id_type=MESH)

    def stage_copies(k):
        copies = []
        for cc in (0, 1):
            at = pl.multiple_of(cc * half_units + k * UNITS, UNITS)
            copies.append(pltpu.make_async_copy(
                gate_hbm.at[:, :, pl.ds(at, UNITS)], stage.at[k, cc, :, :, pl.ds(0, UNITS)], stage_sem.at[k]))
            copies.append(pltpu.make_async_copy(
                up_hbm.at[:, :, pl.ds(at, UNITS)], stage.at[k, cc, :, :, pl.ds(UNITS, UNITS)], stage_sem.at[k]))
        return copies

    def stage_start(k, _):
        for copy in stage_copies(k):
            copy.start()
        return 0

    lax.fori_loop(0, chunks, stage_start, 0)
    grad_cols = pl.ds(pl.multiple_of(c * half_units, half_units), half_units)
    grad_other = pl.ds(pl.multiple_of(other * half_units, half_units), half_units)
    grad_in = pltpu.make_async_copy(grad_hbm.at[:, grad_cols], grad.at[c], in_sem)
    grad_in.start()
    tokens_in = pltpu.make_async_copy(tok_hbm, tok, tok_in)
    tokens_in.start()
    plane_in = pltpu.make_async_copy(own_planes.at[z], planes.at[z], tok_own)

    pl.semaphore_wait(barrier, len(peers))

    my_block = pl.ds(pl.multiple_of(x * chip_rows + c * own_rows + z * part, 16), part)
    across = nz // 2
    early = 4
    offsets = [across]
    for o in range(across - 1, 0, -1):
        offsets += [o, nz - o]

    def send_z(k, _):
        for o in offsets:
            zt = lax.rem(z + o, nz)
            for cc in (c, other):
                pltpu.make_async_remote_copy(
                    stage.at[k, cc, zt], wbuf.at[k, my_block, :], z_send.at[k], z_recv.at[k],
                    (dp - c + cc, zt, y), MESH).start()
        return 0

    other_block = pl.ds(pl.multiple_of(x * chip_rows + other * own_rows + z * part, 16), part)

    def hand_over(k):
        return pltpu.make_async_remote_copy(
            stage.at[k, other, z], wbuf.at[k, my_block, :], d_send.at[k], d_recv.at[k], partner, MESH)

    def ahead(k, way):
        src = stage.at[k, c, z] if way < 2 else wbuf.at[k, other_block, :]
        where = my_block if way < 2 else other_block
        to = right if way % 2 == 0 else left
        return pltpu.make_async_remote_copy(
            src, wbuf.at[k, where, :], f_send.at[way, k], f_recv.at[way, k], (to * 2 + c, z, y), MESH)

    def begin(k, _):
        pltpu.make_async_copy(stage.at[k], stage.at[k], stage_sem.at[k]).wait()
        pltpu.make_async_copy(stage.at[k, c, z], wbuf.at[k, my_block, :], own_sem.at[k]).start()
        hand_over(k).start()
        ahead(k, 0).start()
        ahead(k, 1).start()
        return 0

    def follow(k, _):
        hand_over(k).wait_recv()
        ahead(k, 2).start()
        ahead(k, 3).start()
        return 0

    def dispatch():
        tokens = tok.shape[0]
        expert = lax.broadcasted_iota(jnp.int32, (nz, tokens), 0)
        first, second = ids[0:1, :] == expert, ids[1:2, :] == expert
        named = jnp.where(first | second, 1.0, 0.0)
        factors = weights[...].astype(f32)
        route = jnp.where(first, factors[0:1, :], 0.0) + jnp.where(second, factors[1:2, :], 0.0)
        earlier = (lax.broadcasted_iota(jnp.int32, (tokens, tokens), 0)
                   < lax.broadcasted_iota(jnp.int32, (tokens, tokens), 1))
        before = jnp.dot(named.astype(bf16), jnp.where(earlier, 1.0, 0.0).astype(bf16), preferred_element_type=f32)
        place = jnp.where(named > 0.5, before, -1.0).astype(jnp.int32)
        slot = lax.broadcasted_iota(jnp.int32, (padded, tokens), 0)
        for e in range(nz):
            picked = jnp.where(slot == place[e:e + 1, :], 1.0, 0.0)
            chosen[pl.ds(e * padded, padded), :] = picked.astype(bf16)
            select[pl.ds(e, cap, stride=nz), :] = picked[:cap]
            factor = jnp.sum(picked[:cap] * route[e:e + 1, :], axis=1, keepdims=True)
            own_planes[e, :, feat:] = jnp.broadcast_to(factor, (cap, 128)).astype(bf16)
        tokens_in.wait()
        taken = jnp.dot(chosen[...], tok[...], preferred_element_type=f32).astype(bf16)
        for e in range(nz):
            own_planes[e, :, :feat] = taken[e * padded:e * padded + cap, :]

    def plane_out(o):
        zt = lax.rem(z + o, nz)
        return pltpu.make_async_remote_copy(
            own_planes.at[zt], planes.at[z], tok_send.at[o - 1], tok_recv.at[z], (dp, zt, y), MESH)

    begin(0, 0)
    for part_of in (0, 1):
        lane = pl.ds(part_of * UNITS, UNITS)
        slot = part_of * chunks
        for o in offsets:
            zt = lax.rem(z + o, nz)
            for cc in (c, other):
                pltpu.make_async_remote_copy(
                    stage.at[0, cc, zt, :, lane], wbuf.at[0, my_block, lane], z_send.at[slot], z_recv.at[slot],
                    (dp - c + cc, zt, y), MESH).start()
    lax.fori_loop(1, chunks, begin, 0)
    dispatch()
    lax.fori_loop(0, chunks, follow, 0)
    lax.fori_loop(1, early, send_z, 0)
    plane_in.start()
    for o in offsets:
        plane_out(o).start()
    lax.fori_loop(early, chunks, send_z, 0)

    def to_partner(n, src, dst):
        return pltpu.make_async_remote_copy(src, dst, p_send.at[n], p_recv.at[n], partner, MESH)

    grad_out = to_partner(5, grad_hbm.at[:, grad_other], grad.at[c])
    grad_out.start()

    def rows_of(chip, first, count):
        return pl.ds(pl.multiple_of(chip * chip_rows + first, 16), count)

    def piece_of(k, part_of):
        lane = pl.ds(0, 2 * UNITS) if part_of is None else pl.ds(part_of * UNITS, UNITS)
        slot = k if part_of != 1 else chunks if k == 0 else chunks + 1
        return lane, slot

    def x_copy(k, way, chip, first, count, part_of=None):
        lane, slot = piece_of(k, part_of)
        where = wbuf.at[k, rows_of(chip, first, count), lane]
        to = right if way % 2 == 0 else left
        return pltpu.make_async_remote_copy(
            where, where, x_send.at[way, slot], x_recv.at[way, slot], (to * 2 + c, z, y), MESH)

    n_in = 2 * nz - 2
    runs = []
    size, base = nz // 2, 0
    while size:
        side = lax.rem(z // size, 2)
        runs.append((base + (1 - side) * size, size))
        base = base + side * size
        size //= 2

    def x_start(k, part_of=None):
        for cc in (0, 1):
            for at, size in runs:
                for way in (0, 1):
                    x_copy(k, way, x, cc * own_rows + at * part, size * part, part_of).start()

    def x_wait(k, sems, way, part_of=None):
        lane, slot = piece_of(k, part_of)
        whole = wbuf.at[k, pl.ds(0, n_in * part), lane]
        pltpu.make_async_copy(whole, whole, sems.at[way, slot]).wait()

    def step_own(k):
        whole = wbuf.at[k, pl.ds(0, n_in * part), :]
        pltpu.make_async_copy(whole, whole, z_recv.at[k]).wait()
        pltpu.make_async_copy(stage.at[k, c, z], wbuf.at[k, my_block, :], own_sem.at[k]).wait()
        for part_of in ((0, 1) if k == chunks - 1 else (None,)):
            x_start(k, part_of)

    def step_relay(k, part_of=None):
        if not part_of:
            ahead(k, 0).wait_recv()
            ahead(k, 2).wait_recv()
        x_wait(k, x_recv, 0, part_of)
        x_copy(k, 2, left, 0, own_rows, part_of).start()
        if not part_of:
            ahead(k, 1).wait_recv()
            ahead(k, 3).wait_recv()
        x_wait(k, x_recv, 1, part_of)
        x_copy(k, 3, right, own_rows, own_rows, part_of).start()

    def first_own(part_of):
        whole = wbuf.at[0, pl.ds(0, n_in * part), pl.ds(part_of * UNITS, UNITS)]
        pltpu.make_async_copy(whole, whole, z_recv.at[part_of * chunks]).wait()
        x_start(0, part_of)

    def arrived(k):
        for part_of in (0, 1):
            x_copy(k, 2, far, 0, own_rows, part_of).wait_recv()
            x_copy(k, 3, far, own_rows, own_rows, part_of).wait_recv()

    def cols_of(t):
        return pl.ds(pl.multiple_of(t * feat, 128), feat)

    def y_copy(way, t, first, count):
        where = rows.at[c, pl.ds(first, count), cols_of(t)]
        to = y_right if way % 2 == 0 else y_left
        return pltpu.make_async_remote_copy(where, where, y_send.at[way], y_recv.at[way], (dp, z, to), MESH)

    def share(n, t):
        where = rows.at[c, :, cols_of(t)]
        return to_partner(n, where, where)

    def shared(n, t):
        where = rows.at[other, :, cols_of(t)]
        pltpu.make_async_copy(where, where, p_recv.at[n]).wait()

    def gather_rows():
        plane_in.wait()
        for o in offsets:
            zs = lax.rem(z + o, nz)
            pltpu.make_async_copy(own_planes.at[zs], planes.at[zs], tok_recv.at[zs]).wait()
        for j in range(nz):
            for n in range(lanes + 1):
                spread[n, pl.ds(j, cap, stride=nz), :] = planes[j, :, n * 128:(n + 1) * 128].astype(f32)
        rows[c, :, cols_of(y)] = jnp.concatenate([spread[n] for n in range(lanes)], axis=1).astype(bf16)
        scale[c] = spread[lanes]
        y_copy(0, y, 0, slots).start()
        y_copy(1, y, 0, slots).start()
        share(0, y).start()
        to_partner(4, scale.at[c], scale.at[c]).start()

    def hid_out(k):
        cols = pl.ds(pl.multiple_of(c * half_units + k * UNITS, UNITS), UNITS)
        here = pltpu.make_async_copy(hid.at[k, c], hid_hbm.at[:, cols], hid_sem.at[k])
        there = pltpu.make_async_remote_copy(
            hid.at[k, other], hid_hbm.at[:, cols], hid_send.at[k], hid_recv.at[k], partner, MESH)
        return here, there

    swaps = (y_far, y_right, y_left, y)

    def swap(n):
        return pltpu.make_async_remote_copy(bsend.at[n], brecv.at[n], b_send.at[n], b_recv.at[n], partner, MESH)

    def compute(k):
        @pl.when((k > 0) & (k < chunks - 1))
        def _():
            x_copy(k, 2, far, 0, own_rows).wait_recv()
            x_copy(k, 3, far, own_rows, own_rows).wait_recv()
        at = pl.ds(pl.multiple_of(k * UNITS, UNITS), UNITS)
        both = jnp.dot(rows[...].reshape(2 * slots, rows.shape[2]), wbuf[k], preferred_element_type=f32)
        gate, up = both[:, :UNITS], both[:, UNITS:]
        weight = scale[...].reshape(2 * slots, UNITS)
        sig = jax.nn.sigmoid(gate)
        hidden = (weight * gate * sig * up).astype(bf16)
        hid[k] = hidden.reshape(2, slots, UNITS)
        grad_act = weight * grad[:, :, at].reshape(2 * slots, UNITS).astype(f32)
        gate_grad = (grad_act * up * sig * (1.0 + gate * (1.0 - sig))).astype(bf16)
        up_grad = (grad_act * gate * sig).astype(bf16)
        pairs[:, :UNITS] = gate_grad
        pairs[:, UNITS:] = up_grad
        here, there = hid_out(k)
        here.start()
        there.start()

        def backward(n, _):
            cols = cols_of(lax.rem(y + 2 + 3 * n + 3 * (n // 2) + 2 * (n // 3), ny))
            term = lax.dot_general(pairs[...], wbuf[k, cols, :], (((1,), (1,)), ((), ())), preferred_element_type=f32)
            acc[:, :, cols] += term.reshape(2, slots, feat)

            @pl.when(k == chunks - 1)
            def _():
                bsend[n] = acc[other, :, cols].astype(bf16)
                swap(n).start()
            return 0

        lax.fori_loop(0, ny, backward, 0)

    acc[...] = jnp.zeros_like(acc)
    pltpu.make_async_copy(stage.at[0, c, z], wbuf.at[0, my_block, :], own_sem.at[0]).wait()
    first_own(0)
    first_own(1)
    step_relay(0, 0)
    step_relay(0, 1)
    step_own(1)
    step_own(2)
    step_relay(1)
    step_own(3)
    step_relay(2)
    gather_rows()
    step_relay(3)
    step_own(4)
    y_copy(0, y_left, 0, slots).wait_recv()
    y_copy(2, y_left, 0, half).start()
    share(1, y_left).start()
    y_copy(1, y_right, 0, slots).wait_recv()
    y_copy(3, y_right, half, half).start()
    share(2, y_right).start()
    step_own(5)
    y_copy(2, y_far, 0, half).wait_recv()
    y_copy(3, y_far, half, half).wait_recv()
    share(3, y_far).start()
    grad_in.wait()
    pltpu.make_async_copy(grad_hbm.at[:, grad_other], grad.at[other], p_recv.at[5]).wait()
    pltpu.make_async_copy(scale.at[other], scale.at[other], p_recv.at[4]).wait()
    for n, t in enumerate((y, y_left, y_right, y_far)):
        shared(n, t)

    arrived(0)

    def main(k, _):
        compute(k)

        @pl.when(k == 0)
        def _():
            step_relay(4)
            step_own(6)

        @pl.when(k == 2)
        def _():
            step_relay(5)
            step_own(7)

        @pl.when(k == 4)
        def _():
            step_relay(6)

        @pl.when(k == 5)
        def _():
            step_relay(7, 0)
            step_relay(7, 1)

        @pl.when(k == 6)
        def _():
            arrived(7)
        return 0

    lax.fori_loop(0, chunks, main, 0)

    subs = 2 * pairs_of
    sub = slots // subs
    per = cap // pairs_of

    def piece(kind, n):
        to = y_right if (n + kind) % 2 == 0 else y_left
        at = (kind // 2) * subs + n if kind % 2 == 0 else 2 * subs + n
        return pltpu.make_async_remote_copy(
            ysend.at[at], yrecv.at[at], ys_send.at[at], ys_recv.at[at], (dp, z, to), MESH)

    def got(kind, n):
        at = (kind // 2) * subs + n if kind % 2 == 0 else 2 * subs + n
        piece(kind, n).wait_recv()
        return yrecv[at].astype(f32)

    def pass_on(kind, n, value):
        at = (kind // 2) * subs + n if kind % 2 == 0 else 2 * subs + n
        ysend[at] = value.astype(bf16)
        piece(kind, n).start()

    def mine(order, n):
        rows_n = pl.ds(n * sub, sub)
        return acc[c, rows_n, cols_of(swaps[order])] + brecv[order, rows_n].astype(f32)

    swap(0).wait_recv()
    for n in range(subs):
        pass_on(0, n, mine(0, n))
    swap(1).wait_recv()
    swap(2).wait_recv()
    for g in range(pairs_of):
        for n in (2 * g + 1, 2 * g):
            pass_on(1, n, mine(1 if n % 2 else 2, n))
        for n in (2 * g, 2 * g + 1):
            pass_on(2, n, mine(2 if n % 2 else 1, n) + got(0, n))
    swap(3).wait_recv()

    def give_back(g, o):
        zt = lax.rem(z + o, nz)
        return pltpu.make_async_remote_copy(
            zsend.at[g, zt], back.at[g, z], r_send.at[g, o - 1], r_recv.at[g, z], (dp, zt, y), MESH)

    def keep(g):
        return pltpu.make_async_copy(zsend.at[g, z], back.at[g, z], r_own.at[g])

    for g in range(pairs_of):
        for i in (0, 1):
            n = 2 * g + i
            total = mine(3, n) + got(1, n) + got(2, n)
            for m in range(lanes):
                final[m, pl.ds(i * sub, sub), :] = total[:, m * 128:(m + 1) * 128]
        for j in range(nz):
            zsend[g, j] = jnp.concatenate(
                [final[m, pl.ds(j, per, stride=nz), :] for m in range(lanes)], axis=1).astype(bf16)
        for o in offsets:
            give_back(g, o).start()
        keep(g).start()

    def sent(k, part_of):
        x_wait(k, x_send, 0, part_of)
        x_wait(k, x_send, 1, part_of)
        x_copy(k, 2, left, 0, own_rows, part_of).wait_send()
        x_copy(k, 3, right, own_rows, own_rows, part_of).wait_send()

    for part_of in (0, 1):
        whole = wbuf.at[0, pl.ds(0, n_in * part), pl.ds(part_of * UNITS, UNITS)]
        pltpu.make_async_copy(whole, whole, z_send.at[part_of * chunks]).wait()
        sent(0, part_of)
        sent(chunks - 1, part_of)

    def drain(k, _):
        @pl.when(k > 0)
        def _():
            whole = wbuf.at[k, pl.ds(0, n_in * part), :]
            pltpu.make_async_copy(whole, whole, z_send.at[k]).wait()

        @pl.when((k > 0) & (k < chunks - 1))
        def _():
            sent(k, None)
        hand_over(k).wait_send()
        for way in range(4):
            ahead(k, way).wait_send()
        here, there = hid_out(k)
        here.wait()
        there.wait_send()
        cols = pl.ds(pl.multiple_of(other * half_units + k * UNITS, UNITS), UNITS)
        pltpu.make_async_copy(hid.at[k, other], hid_hbm.at[:, cols], hid_recv.at[k]).wait()
        return 0

    lax.fori_loop(0, chunks, drain, 0)
    for o in offsets:
        plane_out(o).wait_send()
    y_copy(0, y, 0, slots).wait_send()
    y_copy(1, y, 0, slots).wait_send()
    y_copy(2, y_left, 0, half).wait_send()
    y_copy(3, y_right, half, half).wait_send()
    for n, t in enumerate((y, y_left, y_right, y_far)):
        share(n, t).wait_send()
    to_partner(4, scale.at[c], scale.at[c]).wait_send()
    grad_out.wait_send()
    for n in range(4):
        swap(n).wait_send()
    for kind in range(3):
        for n in range(subs):
            piece(kind, n).wait_send()

    result = jnp.zeros(tok_out.shape, f32)
    for g in range(pairs_of):
        keep(g).wait()
        for o in offsets:
            zs = lax.rem(z + o, nz)
            pltpu.make_async_copy(zsend.at[g, zs], back.at[g, zs], r_recv.at[g, zs]).wait()
        for e in range(nz):
            for m in range(lanes):
                spread[m, pl.ds(2 * g * sub + e, per, stride=nz), :] = back[g, e, :, m * 128:(m + 1) * 128].astype(f32)
        rows_g = pl.ds(2 * g * sub, 2 * sub)
        gathered = jnp.concatenate([spread[m, rows_g, :] for m in range(lanes)], axis=1).astype(bf16)
        result += lax.dot_general(select[rows_g, :].astype(bf16), gathered, (((0,), (0,)), ((), ())), preferred_element_type=f32)
    for g in range(pairs_of):
        for o in offsets:
            give_back(g, o).wait_send()
    tok_out[...] = result.astype(bf16)


def stream(nx, nz, ny, cap, ids, weights, tokens, w_gate, w_up, grad):
    slots, hidden = grad.shape
    count, feat = tokens.shape
    padded = -(-cap // 16) * 16
    d = feat * ny
    pairs_of = 9
    chunks = hidden // 2 // UNITS
    part = w_gate.shape[1]
    bf16, f32 = jnp.bfloat16, jnp.float32
    dma = pltpu.SemaphoreType.DMA
    return pl.pallas_call(
        functools.partial(stream_kernel, nx, nz, ny, pairs_of),
        out_shape=(pltpu.VMEM((slots, hidden), bf16), pltpu.VMEM((count, feat), bf16)),
        in_specs=[pl.BlockSpec(memory_space=pltpu.VMEM)] * 2 + [pl.BlockSpec(memory_space=pl.ANY)] * 4,
        out_specs=(pl.BlockSpec(memory_space=pltpu.VMEM), pl.BlockSpec(memory_space=pltpu.VMEM)),
        scratch_shapes=[
            pltpu.VMEM((chunks, 2, nz, part, 2 * UNITS), bf16),
            pltpu.VMEM((chunks, d, 2 * UNITS), bf16),
            pltpu.VMEM((2 * slots, 2 * UNITS), bf16),
            pltpu.VMEM((count, feat), bf16),
            pltpu.VMEM((nz * padded, count), bf16),
            pltpu.VMEM((slots, count), f32),
            pltpu.VMEM((nz, cap, feat + 128), bf16),
            pltpu.VMEM((nz, cap, feat + 128), bf16),
            pltpu.VMEM((feat // 128 + 1, slots, 128), f32),
            pltpu.VMEM((2, slots, d), bf16),
            pltpu.VMEM((2, slots, UNITS), f32),
            pltpu.VMEM((2, slots, hidden // 2), bf16),
            pltpu.VMEM((chunks, 2, slots, UNITS), bf16),
            pltpu.VMEM((2, slots, d), f32),
            pltpu.VMEM((4, slots, feat), bf16),
            pltpu.VMEM((4, slots, feat), bf16),
            pltpu.VMEM((6 * pairs_of, slots // (2 * pairs_of), feat), bf16),
            pltpu.VMEM((6 * pairs_of, slots // (2 * pairs_of), feat), bf16),
            pltpu.VMEM((feat // 128, slots // pairs_of, 128), f32),
            pltpu.VMEM((pairs_of, nz, cap // pairs_of, feat), bf16),
            pltpu.VMEM((pairs_of, nz, cap // pairs_of, feat), bf16),
            dma((chunks,)), dma((chunks,)), dma((chunks,)), dma((chunks,)), dma((4, chunks)), dma((4, chunks)),
            dma((chunks + 1,)), dma((chunks + 1,)),
            dma((4, chunks + 2)), dma((4, chunks + 2)),
            dma(()), dma(()), dma((nz - 1,)), dma((nz,)), dma((4,)), dma((4,)),
            dma(()), dma((6,)), dma((6,)), dma((chunks,)), dma((chunks,)), dma((chunks,)),
            dma((4,)), dma((4,)), dma((6 * pairs_of,)), dma((6 * pairs_of,)),
            dma((pairs_of,)), dma((pairs_of, nz - 1)), dma((pairs_of, nz)),
        ],
        compiler_params=pltpu.CompilerParams(
            collective_id=0, has_side_effects=True, vmem_limit_bytes=62 * 1024 * 1024),
        name="stream",
    )(ids, weights, tokens, w_gate, w_up, grad)


def per_device(nx, nz, ny, tokens, expert_ids, route_weight, w_gate, w_up, grad_hidden):
    slots_cap = grad_hidden.shape[3]
    hidden_part = w_gate.shape[2]
    slots = nz * slots_cap
    grad = grad_hidden.transpose(0, 1, 3, 2, 4).reshape(slots, hidden_part)
    hidden, grad_tokens = stream(nx, nz, ny, slots_cap, expert_ids.T, route_weight.T,
                                 tokens, w_gate, w_up, grad)
    hidden_out = hidden.reshape(1, 1, slots_cap, nz, hidden_part).transpose(0, 1, 3, 2, 4)
    return hidden_out, grad_tokens


def solution(mesh):
    nx, nz, ny = mesh.shape["dp"] // 2, mesh.shape["expert"], mesh.shape["mp"]
    in_specs = (
        P(("dp", "expert"), "mp"),
        P(("dp", "expert"), None),
        P(("dp", "expert"), None),
        P(None, ("dp", "expert"), "mp"),
        P(None, ("dp", "expert"), "mp"),
        P("expert", "dp", None, None, "mp"),
    )
    out_specs = (P("expert", "dp", None, None, "mp"), P(("dp", "expert"), "mp"))
    return jax.shard_map(
        functools.partial(per_device, nx, nz, ny), mesh=mesh, in_specs=in_specs, out_specs=out_specs, check_vma=False
    )
```

```python
import functools

import jax
import jax.numpy as jnp
from jax import lax
from jax.experimental import pallas as pl
from jax.experimental.pallas import tpu as pltpu
from jax.sharding import PartitionSpec as P

MESH = pl.DeviceIdType.MESH
UNITS = 128


def stream_kernel(nx, nz, ny, pairs_of, ids, weights, tok_hbm, gate_hbm, up_hbm, grad_hbm, hid_hbm, tok_out,
                  stage, wbuf, pairs, tok, chosen, select, own_planes, planes, spread, rows, scale, grad, hid, acc, bsend, brecv, ysend, yrecv, final, zsend, back,
                  stage_sem, own_sem, d_send, d_recv, f_send, f_recv, z_send, z_recv, x_send, x_recv, tok_in, tok_own, tok_send, tok_recv, y_send, y_recv,
                  in_sem, p_send, p_recv, hid_sem, hid_send, hid_recv, b_send, b_recv, ys_send, ys_recv,
                  r_own, r_send, r_recv):
    dp, z, y = lax.axis_index("dp"), lax.axis_index("expert"), lax.axis_index("mp")
    x, c = dp // 2, lax.rem(dp, 2)
    other = 1 - c
    left, right = lax.rem(x + nx - 1, nx), lax.rem(x + 1, nx)
    far = lax.rem(x + 2, nx)
    y_left, y_right, y_far = lax.rem(y + ny - 1, ny), lax.rem(y + 1, ny), lax.rem(y + 2, ny)
    chunks = wbuf.shape[0]
    part = gate_hbm.shape[1]
    own_rows = part * nz
    chip_rows = 2 * own_rows
    slots = rows.shape[1]
    half = slots // 2
    cap = planes.shape[1]
    feat = tok_out.shape[1]
    lanes = feat // 128
    padded = chosen.shape[0] // nz
    half_units = chunks * UNITS
    bf16, f32 = jnp.bfloat16, jnp.float32
    partner = (dp - c + other, z, y)

    barrier = pltpu.get_barrier_semaphore()
    peers = [(dp - c + cc, lax.rem(z + o, nz), y) for o in range(1, nz) for cc in (0, 1)]
    peers += [partner, (left * 2 + c, z, y), (right * 2 + c, z, y), (dp, z, y_left), (dp, z, y_right)]
    for peer in peers:
        pl.semaphore_signal(barrier, inc=1, device_id=peer, device_id_type=MESH)

    def stage_copies(k):
        copies = []
        for cc in (0, 1):
            at = pl.multiple_of(cc * half_units + k * UNITS, UNITS)
            copies.append(pltpu.make_async_copy(
                gate_hbm.at[:, :, pl.ds(at, UNITS)], stage.at[k, cc, :, :, pl.ds(0, UNITS)], stage_sem.at[k]))
            copies.append(pltpu.make_async_copy(
                up_hbm.at[:, :, pl.ds(at, UNITS)], stage.at[k, cc, :, :, pl.ds(UNITS, UNITS)], stage_sem.at[k]))
        return copies

    def stage_start(k, _):
        for copy in stage_copies(k):
            copy.start()
        return 0

    lax.fori_loop(0, chunks, stage_start, 0)
    grad_cols = pl.ds(pl.multiple_of(c * half_units, half_units), half_units)
    grad_other = pl.ds(pl.multiple_of(other * half_units, half_units), half_units)
    grad_in = pltpu.make_async_copy(grad_hbm.at[:, grad_cols], grad.at[c], in_sem)
    grad_in.start()
    tokens_in = pltpu.make_async_copy(tok_hbm, tok, tok_in)
    tokens_in.start()
    plane_in = pltpu.make_async_copy(own_planes.at[z], planes.at[z], tok_own)

    pl.semaphore_wait(barrier, len(peers))

    my_block = pl.ds(pl.multiple_of(x * chip_rows + c * own_rows + z * part, 16), part)
    across = nz // 2
    early = 4
    offsets = [across]
    for o in range(across - 1, 0, -1):
        offsets += [o, nz - o]

    def send_z(k, _):
        for o in offsets:
            zt = lax.rem(z + o, nz)
            for cc in (c, other):
                pltpu.make_async_remote_copy(
                    stage.at[k, cc, zt], wbuf.at[k, my_block, :], z_send.at[k], z_recv.at[k],
                    (dp - c + cc, zt, y), MESH).start()
        return 0

    other_block = pl.ds(pl.multiple_of(x * chip_rows + other * own_rows + z * part, 16), part)

    def hand_over(k):
        return pltpu.make_async_remote_copy(
            stage.at[k, other, z], wbuf.at[k, my_block, :], d_send.at[k], d_recv.at[k], partner, MESH)

    def ahead(k, way):
        src = stage.at[k, c, z] if way < 2 else wbuf.at[k, other_block, :]
        where = my_block if way < 2 else other_block
        to = right if way % 2 == 0 else left
        return pltpu.make_async_remote_copy(
            src, wbuf.at[k, where, :], f_send.at[way, k], f_recv.at[way, k], (to * 2 + c, z, y), MESH)

    def begin(k, _):
        pltpu.make_async_copy(stage.at[k], stage.at[k], stage_sem.at[k]).wait()
        pltpu.make_async_copy(stage.at[k, c, z], wbuf.at[k, my_block, :], own_sem.at[k]).start()
        hand_over(k).start()
        ahead(k, 0).start()
        ahead(k, 1).start()
        return 0

    def follow(k, _):
        hand_over(k).wait_recv()
        ahead(k, 2).start()
        ahead(k, 3).start()
        return 0

    def dispatch():
        tokens = tok.shape[0]
        expert = lax.broadcasted_iota(jnp.int32, (nz, tokens), 0)
        first, second = ids[0:1, :] == expert, ids[1:2, :] == expert
        named = jnp.where(first | second, 1.0, 0.0)
        factors = weights[...].astype(f32)
        route = jnp.where(first, factors[0:1, :], 0.0) + jnp.where(second, factors[1:2, :], 0.0)
        earlier = (lax.broadcasted_iota(jnp.int32, (tokens, tokens), 0)
                   < lax.broadcasted_iota(jnp.int32, (tokens, tokens), 1))
        before = jnp.dot(named.astype(bf16), jnp.where(earlier, 1.0, 0.0).astype(bf16), preferred_element_type=f32)
        place = jnp.where(named > 0.5, before, -1.0).astype(jnp.int32)
        slot = lax.broadcasted_iota(jnp.int32, (padded, tokens), 0)
        for e in range(nz):
            picked = jnp.where(slot == place[e:e + 1, :], 1.0, 0.0)
            chosen[pl.ds(e * padded, padded), :] = picked.astype(bf16)
            select[pl.ds(e, cap, stride=nz), :] = picked[:cap]
            factor = jnp.sum(picked[:cap] * route[e:e + 1, :], axis=1, keepdims=True)
            own_planes[e, :, feat:] = jnp.broadcast_to(factor, (cap, 128)).astype(bf16)
        tokens_in.wait()
        taken = jnp.dot(chosen[...], tok[...], preferred_element_type=f32).astype(bf16)
        for e in range(nz):
            own_planes[e, :, :feat] = taken[e * padded:e * padded + cap, :]

    def plane_out(o):
        zt = lax.rem(z + o, nz)
        return pltpu.make_async_remote_copy(
            own_planes.at[zt], planes.at[z], tok_send.at[o - 1], tok_recv.at[z], (dp, zt, y), MESH)

    begin(0, 0)
    for part_of in (0, 1):
        lane = pl.ds(part_of * UNITS, UNITS)
        slot = part_of * chunks
        for o in offsets:
            zt = lax.rem(z + o, nz)
            for cc in (c, other):
                pltpu.make_async_remote_copy(
                    stage.at[0, cc, zt, :, lane], wbuf.at[0, my_block, lane], z_send.at[slot], z_recv.at[slot],
                    (dp - c + cc, zt, y), MESH).start()
    lax.fori_loop(1, chunks, begin, 0)
    lax.fori_loop(0, chunks, follow, 0)
    send_z(1, 0)

    def to_partner(n, src, dst):
        return pltpu.make_async_remote_copy(src, dst, p_send.at[n], p_recv.at[n], partner, MESH)

    grad_out = to_partner(5, grad_hbm.at[:, grad_other], grad.at[c])

    def rows_of(chip, first, count):
        return pl.ds(pl.multiple_of(chip * chip_rows + first, 16), count)

    def piece_of(k, part_of):
        lane = pl.ds(0, 2 * UNITS) if part_of is None else pl.ds(part_of * UNITS, UNITS)
        slot = k if part_of != 1 else chunks if k == 0 else chunks + 1
        return lane, slot

    def x_copy(k, way, chip, first, count, part_of=None):
        lane, slot = piece_of(k, part_of)
        where = wbuf.at[k, rows_of(chip, first, count), lane]
        to = right if way % 2 == 0 else left
        return pltpu.make_async_remote_copy(
            where, where, x_send.at[way, slot], x_recv.at[way, slot], (to * 2 + c, z, y), MESH)

    n_in = 2 * nz - 2
    runs = []
    size, base = nz // 2, 0
    while size:
        side = lax.rem(z // size, 2)
        runs.append((base + (1 - side) * size, size))
        base = base + side * size
        size //= 2

    def x_start(k, part_of=None):
        for cc in (0, 1):
            for at, size in runs:
                for way in (0, 1):
                    x_copy(k, way, x, cc * own_rows + at * part, size * part, part_of).start()

    def x_wait(k, sems, way, part_of=None):
        lane, slot = piece_of(k, part_of)
        whole = wbuf.at[k, pl.ds(0, n_in * part), lane]
        pltpu.make_async_copy(whole, whole, sems.at[way, slot]).wait()

    def step_own(k):
        whole = wbuf.at[k, pl.ds(0, n_in * part), :]
        pltpu.make_async_copy(whole, whole, z_recv.at[k]).wait()
        pltpu.make_async_copy(stage.at[k, c, z], wbuf.at[k, my_block, :], own_sem.at[k]).wait()
        for part_of in ((0, 1) if k == chunks - 1 else (None,)):
            x_start(k, part_of)

    def step_relay(k, part_of=None):
        if not part_of:
            ahead(k, 0).wait_recv()
            ahead(k, 2).wait_recv()
        x_wait(k, x_recv, 0, part_of)
        x_copy(k, 2, left, 0, own_rows, part_of).start()
        if not part_of:
            ahead(k, 1).wait_recv()
            ahead(k, 3).wait_recv()
        x_wait(k, x_recv, 1, part_of)
        x_copy(k, 3, right, own_rows, own_rows, part_of).start()

    def first_own(part_of):
        whole = wbuf.at[0, pl.ds(0, n_in * part), pl.ds(part_of * UNITS, UNITS)]
        pltpu.make_async_copy(whole, whole, z_recv.at[part_of * chunks]).wait()
        x_start(0, part_of)

    def arrived(k):
        for part_of in (0, 1):
            x_copy(k, 2, far, 0, own_rows, part_of).wait_recv()
            x_copy(k, 3, far, own_rows, own_rows, part_of).wait_recv()

    def cols_of(t):
        return pl.ds(pl.multiple_of(t * feat, 128), feat)

    def y_copy(way, t, first, count):
        where = rows.at[c, pl.ds(first, count), cols_of(t)]
        to = y_right if way % 2 == 0 else y_left
        return pltpu.make_async_remote_copy(where, where, y_send.at[way], y_recv.at[way], (dp, z, to), MESH)

    def share(n, t):
        where = rows.at[c, :, cols_of(t)]
        return to_partner(n, where, where)

    def shared(n, t):
        where = rows.at[other, :, cols_of(t)]
        pltpu.make_async_copy(where, where, p_recv.at[n]).wait()

    def gather_rows():
        plane_in.wait()
        for o in offsets:
            zs = lax.rem(z + o, nz)
            pltpu.make_async_copy(own_planes.at[zs], planes.at[zs], tok_recv.at[zs]).wait()
        for j in range(nz):
            for n in range(lanes + 1):
                spread[n, pl.ds(j, cap, stride=nz), :] = planes[j, :, n * 128:(n + 1) * 128].astype(f32)
        rows[c, :, cols_of(y)] = jnp.concatenate([spread[n] for n in range(lanes)], axis=1).astype(bf16)
        scale[c] = spread[lanes]
        y_copy(0, y, 0, slots).start()
        y_copy(1, y, 0, slots).start()
        share(0, y).start()
        to_partner(4, scale.at[c], scale.at[c]).start()

    def hid_out(k):
        cols = pl.ds(pl.multiple_of(c * half_units + k * UNITS, UNITS), UNITS)
        here = pltpu.make_async_copy(hid.at[k, c], hid_hbm.at[:, cols], hid_sem.at[k])
        there = pltpu.make_async_remote_copy(
            hid.at[k, other], hid_hbm.at[:, cols], hid_send.at[k], hid_recv.at[k], partner, MESH)
        return here, there

    swaps = (y_far, y_right, y_left, y)

    def swap(n):
        return pltpu.make_async_remote_copy(bsend.at[n], brecv.at[n], b_send.at[n], b_recv.at[n], partner, MESH)

    def activate(k, both):
        at = pl.ds(pl.multiple_of(k * UNITS, UNITS), UNITS)
        gate, up = both[:, :UNITS], both[:, UNITS:]
        weight = scale[...].reshape(2 * slots, UNITS)
        sig = jax.nn.sigmoid(gate)
        hidden = (weight * gate * sig * up).astype(bf16)
        hid[k] = hidden.reshape(2, slots, UNITS)
        grad_act = weight * grad[:, :, at].reshape(2 * slots, UNITS).astype(f32)
        gate_grad = (grad_act * up * sig * (1.0 + gate * (1.0 - sig))).astype(bf16)
        up_grad = (grad_act * gate * sig).astype(bf16)
        pairs[:, :UNITS] = gate_grad
        pairs[:, UNITS:] = up_grad
        here, there = hid_out(k)
        here.start()
        there.start()

    def backward(k, n):
        cols = cols_of(lax.rem(y + 2 + 3 * n + 3 * (n // 2) + 2 * (n // 3), ny))
        term = lax.dot_general(pairs[...], wbuf[k, cols, :], (((1,), (1,)), ((), ())), preferred_element_type=f32)
        acc[:, :, cols] += term.reshape(2, slots, feat)
        return cols

    def backward_step(k):
        def step(n, _):
            backward(k, n)
            return 0
        return step

    def backward_last(n, _):
        cols = backward(chunks - 1, n)
        bsend[n] = acc[other, :, cols].astype(bf16)
        swap(n).start()
        return 0

    def compute(k):
        @pl.when(k > 0)
        def _():
            x_copy(k, 2, far, 0, own_rows).wait_recv()
            x_copy(k, 3, far, own_rows, own_rows).wait_recv()
        activate(k, jnp.dot(rows[...].reshape(2 * slots, rows.shape[2]), wbuf[k], preferred_element_type=f32))
        lax.fori_loop(0, ny, backward_step(k), 0)

    def forward_part(k, chip):
        which = pl.ds(pl.multiple_of(chip * chip_rows, 128), chip_rows)
        return jnp.dot(rows[:, :, which].reshape(2 * slots, chip_rows), wbuf[k, which, :], preferred_element_type=f32)

    dispatch()
    pltpu.make_async_copy(stage.at[0, c, z], wbuf.at[0, my_block, :], own_sem.at[0]).wait()
    first_own(0)
    first_own(1)
    lax.fori_loop(2, early, send_z, 0)
    plane_in.start()
    for o in offsets:
        plane_out(o).start()
    step_relay(0, 0)
    step_relay(0, 1)
    step_own(1)
    lax.fori_loop(early, chunks, send_z, 0)
    grad_out.start()
    acc[...] = jnp.zeros_like(acc)
    step_own(2)
    step_relay(1)
    step_own(3)
    step_relay(2)
    gather_rows()
    step_relay(3)
    step_own(4)
    y_copy(0, y_left, 0, slots).wait_recv()
    y_copy(2, y_left, 0, half).start()
    share(1, y_left).start()
    y_copy(1, y_right, 0, slots).wait_recv()
    y_copy(3, y_right, half, half).start()
    share(2, y_right).start()
    step_own(5)
    y_copy(2, y_far, 0, half).wait_recv()
    y_copy(3, y_far, half, half).wait_recv()
    share(3, y_far).start()
    grad_in.wait()
    pltpu.make_async_copy(grad_hbm.at[:, grad_other], grad.at[other], p_recv.at[5]).wait()
    pltpu.make_async_copy(scale.at[other], scale.at[other], p_recv.at[4]).wait()
    for n, t in enumerate((y, y_left, y_right, y_far)):
        shared(n, t)

    arrived(0)

    def main(k, _):
        compute(k)

        @pl.when(k == 0)
        def _():
            step_relay(4)
            step_own(6)

        @pl.when(k == 2)
        def _():
            step_relay(5)
            step_own(7)

        @pl.when(k == 4)
        def _():
            step_relay(6)

        @pl.when(k == 5)
        def _():
            step_relay(7, 0)
            step_relay(7, 1)
        return 0

    lax.fori_loop(0, chunks - 1, main, 0)
    last = chunks - 1
    near = forward_part(last, x) + forward_part(last, left) + forward_part(last, right)
    arrived(last)
    activate(last, near + forward_part(last, far))

    subs = 2 * pairs_of
    sub = slots // subs
    per = cap // pairs_of

    def piece(kind, n):
        to = y_right if (n + kind) % 2 == 0 else y_left
        at = (kind // 2) * subs + n if kind % 2 == 0 else 2 * subs + n
        return pltpu.make_async_remote_copy(
            ysend.at[at], yrecv.at[at], ys_send.at[at], ys_recv.at[at], (dp, z, to), MESH)

    def got(kind, n):
        at = (kind // 2) * subs + n if kind % 2 == 0 else 2 * subs + n
        piece(kind, n).wait_recv()
        return yrecv[at].astype(f32)

    def pass_on(kind, n, value):
        at = (kind // 2) * subs + n if kind % 2 == 0 else 2 * subs + n
        ysend[at] = value.astype(bf16)
        piece(kind, n).start()

    def mine(order, n):
        rows_n = pl.ds(n * sub, sub)
        return acc[c, rows_n, cols_of(swaps[order])] + brecv[order, rows_n].astype(f32)

    lax.fori_loop(0, 2, backward_last, 0)
    swap(0).wait_recv()
    for n in range(subs):
        pass_on(0, n, mine(0, n))
    lax.fori_loop(2, ny, backward_last, 0)
    swap(1).wait_recv()
    swap(2).wait_recv()
    for g in range(pairs_of):
        for n in (2 * g + 1, 2 * g):
            pass_on(1, n, mine(1 if n % 2 else 2, n))
        for n in (2 * g, 2 * g + 1):
            pass_on(2, n, mine(2 if n % 2 else 1, n) + got(0, n))
    swap(3).wait_recv()

    def give_back(g, o):
        zt = lax.rem(z + o, nz)
        return pltpu.make_async_remote_copy(
            zsend.at[g, zt], back.at[g, z], r_send.at[g, o - 1], r_recv.at[g, z], (dp, zt, y), MESH)

    def keep(g):
        return pltpu.make_async_copy(zsend.at[g, z], back.at[g, z], r_own.at[g])

    def absorb(g):
        keep(g).wait()
        for o in offsets:
            zs = lax.rem(z + o, nz)
            pltpu.make_async_copy(zsend.at[g, zs], back.at[g, zs], r_recv.at[g, zs]).wait()
        for e in range(nz):
            for m in range(lanes):
                spread[m, pl.ds(2 * g * sub + e, per, stride=nz), :] = back[g, e, :, m * 128:(m + 1) * 128].astype(f32)

    behind = 4
    for g in range(pairs_of):
        for i in (0, 1):
            n = 2 * g + i
            total = mine(3, n) + got(1, n) + got(2, n)
            for m in range(lanes):
                final[m, pl.ds(i * sub, sub), :] = total[:, m * 128:(m + 1) * 128]
        for j in range(nz):
            zsend[g, j] = jnp.concatenate(
                [final[m, pl.ds(j, per, stride=nz), :] for m in range(lanes)], axis=1).astype(bf16)
        for o in offsets:
            give_back(g, o).start()
        keep(g).start()
        if g >= behind:
            absorb(g - behind)

    def sent(k, part_of):
        x_wait(k, x_send, 0, part_of)
        x_wait(k, x_send, 1, part_of)
        x_copy(k, 2, left, 0, own_rows, part_of).wait_send()
        x_copy(k, 3, right, own_rows, own_rows, part_of).wait_send()

    for part_of in (0, 1):
        whole = wbuf.at[0, pl.ds(0, n_in * part), pl.ds(part_of * UNITS, UNITS)]
        pltpu.make_async_copy(whole, whole, z_send.at[part_of * chunks]).wait()
        sent(0, part_of)
        sent(chunks - 1, part_of)

    def drain(k, _):
        @pl.when(k > 0)
        def _():
            whole = wbuf.at[k, pl.ds(0, n_in * part), :]
            pltpu.make_async_copy(whole, whole, z_send.at[k]).wait()

        @pl.when((k > 0) & (k < chunks - 1))
        def _():
            sent(k, None)
        hand_over(k).wait_send()
        for way in range(4):
            ahead(k, way).wait_send()
        here, there = hid_out(k)
        here.wait()
        there.wait_send()
        cols = pl.ds(pl.multiple_of(other * half_units + k * UNITS, UNITS), UNITS)
        pltpu.make_async_copy(hid.at[k, other], hid_hbm.at[:, cols], hid_recv.at[k]).wait()
        return 0

    lax.fori_loop(0, chunks, drain, 0)
    for o in offsets:
        plane_out(o).wait_send()
    y_copy(0, y, 0, slots).wait_send()
    y_copy(1, y, 0, slots).wait_send()
    y_copy(2, y_left, 0, half).wait_send()
    y_copy(3, y_right, half, half).wait_send()
    for n, t in enumerate((y, y_left, y_right, y_far)):
        share(n, t).wait_send()
    to_partner(4, scale.at[c], scale.at[c]).wait_send()
    grad_out.wait_send()
    for n in range(4):
        swap(n).wait_send()
    for kind in range(3):
        for n in range(subs):
            piece(kind, n).wait_send()

    for g in range(pairs_of - behind, pairs_of):
        absorb(g)
    gathered = jnp.concatenate([spread[m] for m in range(lanes)], axis=1).astype(bf16)
    tok_out[...] = lax.dot_general(select[...].astype(bf16), gathered, (((0,), (0,)), ((), ())),
                                   preferred_element_type=f32).astype(bf16)
    for g in range(pairs_of):
        for o in offsets:
            give_back(g, o).wait_send()


def stream(nx, nz, ny, cap, ids, weights, tokens, w_gate, w_up, grad):
    slots, hidden = grad.shape
    count, feat = tokens.shape
    padded = -(-cap // 16) * 16
    d = feat * ny
    pairs_of = 9
    chunks = hidden // 2 // UNITS
    part = w_gate.shape[1]
    bf16, f32 = jnp.bfloat16, jnp.float32
    dma = pltpu.SemaphoreType.DMA
    return pl.pallas_call(
        functools.partial(stream_kernel, nx, nz, ny, pairs_of),
        out_shape=(pltpu.VMEM((slots, hidden), bf16), pltpu.VMEM((count, feat), bf16)),
        in_specs=[pl.BlockSpec(memory_space=pltpu.VMEM)] * 2 + [pl.BlockSpec(memory_space=pl.ANY)] * 4,
        out_specs=(pl.BlockSpec(memory_space=pltpu.VMEM), pl.BlockSpec(memory_space=pltpu.VMEM)),
        scratch_shapes=[
            pltpu.VMEM((chunks, 2, nz, part, 2 * UNITS), bf16),
            pltpu.VMEM((chunks, d, 2 * UNITS), bf16),
            pltpu.VMEM((2 * slots, 2 * UNITS), bf16),
            pltpu.VMEM((count, feat), bf16),
            pltpu.VMEM((nz * padded, count), bf16),
            pltpu.VMEM((slots, count), f32),
            pltpu.VMEM((nz, cap, feat + 128), bf16),
            pltpu.VMEM((nz, cap, feat + 128), bf16),
            pltpu.VMEM((feat // 128 + 1, slots, 128), f32),
            pltpu.VMEM((2, slots, d), bf16),
            pltpu.VMEM((2, slots, UNITS), f32),
            pltpu.VMEM((2, slots, hidden // 2), bf16),
            pltpu.VMEM((chunks, 2, slots, UNITS), bf16),
            pltpu.VMEM((2, slots, d), f32),
            pltpu.VMEM((4, slots, feat), bf16),
            pltpu.VMEM((4, slots, feat), bf16),
            pltpu.VMEM((6 * pairs_of, slots // (2 * pairs_of), feat), bf16),
            pltpu.VMEM((6 * pairs_of, slots // (2 * pairs_of), feat), bf16),
            pltpu.VMEM((feat // 128, slots // pairs_of, 128), f32),
            pltpu.VMEM((pairs_of, nz, cap // pairs_of, feat), bf16),
            pltpu.VMEM((pairs_of, nz, cap // pairs_of, feat), bf16),
            dma((chunks,)), dma((chunks,)), dma((chunks,)), dma((chunks,)), dma((4, chunks)), dma((4, chunks)),
            dma((chunks + 1,)), dma((chunks + 1,)),
            dma((4, chunks + 2)), dma((4, chunks + 2)),
            dma(()), dma(()), dma((nz - 1,)), dma((nz,)), dma((4,)), dma((4,)),
            dma(()), dma((6,)), dma((6,)), dma((chunks,)), dma((chunks,)), dma((chunks,)),
            dma((4,)), dma((4,)), dma((6 * pairs_of,)), dma((6 * pairs_of,)),
            dma((pairs_of,)), dma((pairs_of, nz - 1)), dma((pairs_of, nz)),
        ],
        compiler_params=pltpu.CompilerParams(
            collective_id=0, has_side_effects=True, vmem_limit_bytes=62 * 1024 * 1024),
        name="stream",
    )(ids, weights, tokens, w_gate, w_up, grad)


def per_device(nx, nz, ny, tokens, expert_ids, route_weight, w_gate, w_up, grad_hidden):
    slots_cap = grad_hidden.shape[3]
    hidden_part = w_gate.shape[2]
    slots = nz * slots_cap
    grad = grad_hidden.transpose(0, 1, 3, 2, 4).reshape(slots, hidden_part)
    hidden, grad_tokens = stream(nx, nz, ny, slots_cap, expert_ids.T, route_weight.T,
                                 tokens, w_gate, w_up, grad)
    hidden_out = hidden.reshape(1, 1, slots_cap, nz, hidden_part).transpose(0, 1, 3, 2, 4)
    return hidden_out, grad_tokens


def solution(mesh):
    nx, nz, ny = mesh.shape["dp"] // 2, mesh.shape["expert"], mesh.shape["mp"]
    in_specs = (
        P(("dp", "expert"), "mp"),
        P(("dp", "expert"), None),
        P(("dp", "expert"), None),
        P(None, ("dp", "expert"), "mp"),
        P(None, ("dp", "expert"), "mp"),
        P("expert", "dp", None, None, "mp"),
    )
    out_specs = (P("expert", "dp", None, None, "mp"), P(("dp", "expert"), "mp"))
    return jax.shard_map(
        functools.partial(per_device, nx, nz, ny), mesh=mesh, in_specs=in_specs, out_specs=out_specs, check_vma=False
    )
```
